256 devices in a mesh: seq: 32 (over z_hi, x, core), exp: 8 (over z_lo, y).
Axes of the slice: x: 4, y: 4, z: 8 (z_hi: 4, z_lo: 2; z = z_hi * 2 + z_lo), core: 2. Of those that a mesh axis runs over, the one named last changes fastest.
Arguments:
- tokens: bfloat16 [4096, 2304], P('seq'), may hold values from -6 to 6
- norm_gain: bfloat16 [2304], replicated, may hold values from 0.099609375 to 1.8984375
- w_qkv: bfloat16 [2304, 3, 2048], P(None, None, 'exp'), may hold values from -12 to 12
- w_out: bfloat16 [2048, 2304], P('exp'), may hold values from -0.125 to 0.125
- moe_gain: bfloat16 [2304], replicated, may hold values from 0.099609375 to 1.8984375
- w_router: bfloat16 [2304, 8], replicated, may hold values from -0.25 to 0.25
- gate_up: bfloat16 [8, 2, 2304, 5760], P('exp', None, None, 'seq'), may hold values from -0.125 to 0.125
- w_down: bfloat16 [8, 5760, 2304], P('exp', 'seq'), may hold values from -0.078125 to 0.078125
- lengths: int32 [4], replicated, may hold values from 1 to 3072, as said below
- blocks_seen: int32 [32, 32], P('seq'), may hold values from 0 to 1, as said below
- expert_ids: int32 [4096, 2], P(('seq', 'exp')), may hold values from 0 to 7, all different within a row; in each aligned block of 16 rows (0 to 15, 16 to 31, ...) at most 8 rows name the same one
- old_place: int32 [8], replicated, may hold values from 0 to 7, each once
- new_place: int32 [8], replicated, may hold values from 0 to 7, each once
Outputs:
- layer_out: bfloat16 [4096, 2304], P(('seq', 'exp'))
- new_gate_up: bfloat16 [8, 2, 2304, 5760], P('exp', None, None, 'seq')
- new_down: bfloat16 [8, 5760, 2304], P('exp', 'seq')
The draws below stay inside these ranges and needn't reach their ends.
Inputs may be any that keep to these rules, and one draw needn't show every extreme that they name: `lengths`: positive, summing to 4096, the largest exactly 3072. `blocks_seen`: 1 on the diagonal; 0 above it and wherever no sequence has tokens in both blocks; elsewhere 0 or 1. `expert_ids`: the two experts of a token differ; among the 16 tokens of one device no expert is named more than 8 times, and in some devices one expert exactly 8 times. `old_place`: a permutation of the experts. `new_place`: a permutation of the experts.
All inputs are finite; a program needn't handle non-finite values.
Results may differ from the reference program's by a relative error of at most 0.023.
Values may be sent and summed in bfloat16 or wider, within the bound.
No kernel may reach another device: no remote copies, remote signals or barrier semaphores. Data moves between devices by JAX's collectives and lax.ppermute only.
A program may use at most 128 MiB of HBM per device.

```python
import math
import jax
import jax.numpy as jnp
import numpy as np
from jax import lax

D = 2304
FF = 5760
HEAD_DIM = 64
TOP = 2
HEADS = 32
SEQS = 4
TOK_DEV = 128
EXPERTS = 8
TOKENS = 4096
BLOCKS = 32
TOK_SHARD = 16
MOST_LEN = 3072
CAP = 8
N_SEQ = 32
N_EXP = 8


def doc_lengths(key):
    local_key = jax.random.fold_in(key, 7)
    first_key, second_key = jax.random.split(local_key)
    widths = jax.random.randint(first_key, (SEQS - 1,), 1000, 2001)
    spare = TOKENS - MOST_LEN - (SEQS - 1)
    running = jnp.cumsum(widths, dtype=jnp.int32)
    cuts = spare * running // running[-1]
    parts = 1 + jnp.diff(jnp.concatenate([jnp.zeros((1,), jnp.int32), cuts.astype(jnp.int32)]))
    whole = jnp.concatenate([jnp.full((1,), MOST_LEN, jnp.int32), parts.astype(jnp.int32)])
    offset = jax.random.randint(second_key, (), 0, SEQS)
    return jnp.roll(whole, offset)


def draw_lengths(key, part):
    return doc_lengths(key)


def draw_blocks_seen(key, part):
    seq_lengths = doc_lengths(key)
    ending = jnp.cumsum(seq_lengths, dtype=jnp.int32)
    block_range = jnp.arange(BLOCKS, dtype=jnp.int32)
    first_rows = block_range * TOK_DEV
    last_rows = first_rows + TOK_DEV - 1
    doc_first = jnp.sum((ending[None, :] <= first_rows[:, None]).astype(jnp.int32), axis=1)
    doc_last = jnp.sum((ending[None, :] <= last_rows[:, None]).astype(jnp.int32), axis=1)
    possible = (block_range[None, :] < block_range[:, None]) & (doc_last[None, :] == doc_first[:, None])
    keeping = jax.random.randint(jax.random.fold_in(key, 9), (BLOCKS, BLOCKS), 0, 3) == 0
    diagonal = block_range[:, None] == block_range[None, :]
    return (diagonal | possible & keeping).astype(jnp.int32)


def draw_tokens(key, part):
    first_key = jax.random.fold_in(jax.random.fold_in(key, 3), 0)
    drawn = jax.random.normal(first_key, (TOKENS, D), jnp.float32)
    return jnp.clip(drawn, -6.0, 6.0).astype(jnp.bfloat16)


def draw_w_qkv(key, part):
    columns = HEADS * HEAD_DIM
    drawn = jnp.clip(jax.random.normal(jax.random.fold_in(key, 5), (D, 3, columns), jnp.float32), -6.0, 6.0) / math.sqrt(D)
    return drawn.astype(jnp.bfloat16)


def block_scale(rng, shape, pieces, least, top_value):
    level, own = 1.0, jax.random.fold_in(rng, 6)
    for dim, blocks in pieces:
        heights = jnp.exp(jax.random.uniform(jax.random.fold_in(own, dim), (blocks,), jnp.float32, least / len(pieces), top_value / len(pieces)))
        level = level * jnp.repeat(heights, shape[dim] // blocks).reshape([-1 if axis == dim else 1 for axis in range(len(shape))])
    return level


def routed_block(own_key, own, number, rows, number_of, top, limit, lean):
    ranking = jax.random.permutation(own_key, number_of)
    packed, ordinary = portions_of(number_of, rows * top, limit, lean, True), portions_of(number_of, rows * top, limit, lean, False)
    places = jnp.arange(number_of)

    def named(sizes, turn):
        used = int((sizes > 0).sum())
        fixed = max(1, used // 4)
        shifted = fixed + (places - fixed + turn * (used - fixed)) % max(1, number_of - fixed)
        return jnp.zeros((number_of,), jnp.int32).at[ranking[jnp.where(places < fixed, places, shifted)]].set(jnp.asarray(sizes, jnp.int32))

    sizes = jnp.where(number % 4 == 0, named(packed, number // 4), named(ordinary, number - number // 4 - 1))
    mixed = jax.random.permutation(jax.random.fold_in(own, 3), number_of)
    giver, receiver = mixed[0:number_of // 2 * 2:2], mixed[1:number_of // 2 * 2:2]
    slack = jnp.minimum(sizes[giver] - 1, limit - sizes[receiver]) // 2
    slack = jnp.where((giver == ranking[0]) | (receiver == ranking[0]) | (sizes[receiver] == 0), 0, jnp.maximum(slack, 0))
    shifted = jax.random.randint(jax.random.fold_in(own, 4), (number_of // 2,), 0, 1 << 20) % (slack + 1)
    sizes = sizes.at[giver].add(-shifted).at[receiver].add(shifted)
    labels = jnp.searchsorted(jnp.cumsum(sizes), jnp.arange(rows * top), side="right").astype(jnp.int32)
    grid = labels.reshape(top, rows).T
    grid = grid[jax.random.permutation(jax.random.fold_in(own, 1), rows)]
    turn = jax.random.randint(jax.random.fold_in(own, 2), (rows, 1), 0, top)
    return jnp.take_along_axis(grid, (jnp.arange(top)[None, :] + turn) % top, axis=1)


def portions_of(count, total, bound, slope, full):
    loads = [(1 << 20) // math.isqrt(grade ** slope) + 1 for grade in range(1, count + 1)]
    largest = bound if full else min(bound, max(-(-total // count), total * loads[0] // sum(loads)))
    least = 1 if total - largest >= count - 1 else 0
    counts, rest = [largest] + [least] * (count - 1), total - largest - least * (count - 1)
    while rest > 0:
        free = [i for i in range(1, count) if counts[i] < largest] or [i for i in range(1, count) if counts[i] < bound]
        pool, left = sum([loads[i] for i in free]), rest
        for i in free:
            addition = min(bound - counts[i], max(1, left * loads[i] // pool), rest)
            counts[i] = counts[i] + addition
            rest = rest - addition
    return np.array(counts)


def bell_draw(key, dims, deviation, bound, pieces=(), kind=jnp.bfloat16):
    factor_of = block_scale(key, dims, pieces, -0.22, 0.18) if pieces else 1.0
    values = jax.random.normal(key, dims, jnp.float32) * deviation * factor_of
    return jnp.minimum(jnp.maximum(values, -bound), bound).astype(kind)


def setup_inputs(seed: int = 0) -> dict:
    splits = jax.random.split(jax.random.key(seed), 14)
    tokens = draw_tokens(jax.random.fold_in(splits[13], 71), 0)
    norm_gain = jnp.clip(1.0 + 0.18 * jax.random.normal(splits[1], (D,), jnp.float32), 0.099609375, 1.8984375).astype(jnp.bfloat16)
    w_qkv = draw_w_qkv(jax.random.fold_in(splits[13], 71), 0)
    w_out = bell_draw(splits[3], (HEADS * HEAD_DIM, D), (HEADS * HEAD_DIM) ** -0.5, 0.125, ((0, 8),))
    moe_gain = jnp.clip(1.0 + 0.18 * jax.random.normal(splits[4], (D,), jnp.float32), 0.099609375, 1.8984375).astype(jnp.bfloat16)
    w_router = bell_draw(splits[5], (D, EXPERTS), (D // 4) ** -0.5, 0.25)
    gate_up = bell_draw(splits[6], (EXPERTS, 2, D, FF), D ** -0.5, 0.125, ((0, 8), (3, 32)))
    w_down = bell_draw(splits[7], (EXPERTS, FF, D), FF ** -0.5, 0.078125, ((0, 8), (1, 32)))
    lengths = draw_lengths(jax.random.fold_in(splits[13], 71), 0)
    blocks_seen = draw_blocks_seen(jax.random.fold_in(splits[13], 71), 0)
    expert_ids_keys = jax.random.split(jax.random.fold_in(splits[10], 1), TOKENS // TOK_SHARD)
    expert_ids_turns = jax.random.permutation(jax.random.fold_in(splits[10], 3), TOKENS // TOK_SHARD)
    expert_ids = jax.vmap(lambda own, number: routed_block(jax.random.fold_in(splits[10], 2), own, number, TOK_SHARD, EXPERTS, TOP, CAP, 2))(expert_ids_keys, expert_ids_turns).reshape((TOKENS, TOP))
    old_place = jax.random.permutation(splits[11], EXPERTS).astype(jnp.int32)
    new_place = jax.random.permutation(splits[12], EXPERTS).astype(jnp.int32)
    return {"tokens": tokens, "norm_gain": norm_gain, "w_qkv": w_qkv, "w_out": w_out, "moe_gain": moe_gain, "w_router": w_router, "gate_up": gate_up, "w_down": w_down, "lengths": lengths, "blocks_seen": blocks_seen, "expert_ids": expert_ids, "old_place": old_place, "new_place": new_place}


epsilon = 1e-05
masked_score = -1e+30

def rms_scale(values_in, gain):
    widened = values_in.astype(jnp.float32)
    inverse = lax.rsqrt(lax.optimization_barrier(jnp.mean(widened * widened, axis=-1, keepdims=True)) + epsilon)
    return widened * inverse * gain.astype(jnp.float32)

def rotate(vectors, angle_base):
    halfway = vectors.shape[-1] // 2
    spacing = jnp.arange(halfway, dtype=jnp.float32) / halfway
    freqs_all = jnp.exp(-jnp.log(10000.0) * spacing)
    angles = angle_base[:, None] * freqs_all[None, :]
    cosine = jnp.cos(angles)[:, None, :]
    sine_part = jnp.sin(angles)[:, None, :]
    leading = vectors[..., :halfway]
    trailing = vectors[..., halfway:]
    return jnp.concatenate([leading * cosine - trailing * sine_part, trailing * cosine + leading * sine_part], axis=-1)

def doc_layout(seq_lengths, row_ids):
    ending = jnp.cumsum(seq_lengths, dtype=jnp.int32)
    passed = (ending[None, :] <= row_ids[:, None]).astype(jnp.int32)
    doc_ids = lax.optimization_barrier(jnp.sum(passed, axis=1, dtype=jnp.int32))
    starting = lax.optimization_barrier(jnp.sum(passed * seq_lengths[None, :], axis=1, dtype=jnp.int32))
    return (doc_ids, row_ids - starting)

def reference(tokens, norm_gain, w_qkv, w_out, moe_gain, w_router, gate_up, w_down, lengths, blocks_seen, expert_ids, old_place, new_place):
    row_ids = jnp.arange(TOKENS, dtype=jnp.int32)
    doc_ids, places = doc_layout(lengths, row_ids)
    normed = rms_scale(tokens, norm_gain).astype(jnp.bfloat16)
    projected = jnp.dot(normed, w_qkv.reshape(D, 3 * HEADS * HEAD_DIM), preferred_element_type=jnp.float32)
    projected = projected.reshape(TOKENS, 3, HEADS, HEAD_DIM)
    angle_rows = places.astype(jnp.float32)
    queries = rotate(projected[:, 0], angle_rows).astype(jnp.bfloat16)
    key_all = rotate(projected[:, 1], angle_rows).astype(jnp.bfloat16)
    value_all = projected[:, 2].astype(jnp.bfloat16)
    block_ids = row_ids // TOK_DEV
    allowed = (doc_ids[:, None] == doc_ids[None, :]) & (row_ids[None, :] <= row_ids[:, None]) & (blocks_seen[block_ids[:, None], block_ids[None, :]] == 1)
    score_scale = HEAD_DIM ** (-0.5)

    def one_head(operands):
        query_head, key_head, value_head = operands
        scores = jnp.dot(query_head, key_head.T, preferred_element_type=jnp.float32) * score_scale
        scores = jnp.where(allowed, scores, masked_score)
        largest = lax.optimization_barrier(jnp.max(scores, axis=1, keepdims=True))
        weights = jnp.where(allowed, jnp.exp(scores - largest), 0.0)
        totals = lax.optimization_barrier(jnp.sum(weights, axis=1, keepdims=True))
        mixed_rows = jnp.dot(weights.astype(jnp.bfloat16), value_head, preferred_element_type=jnp.float32)
        return (mixed_rows / totals).astype(jnp.bfloat16)
    attended = lax.map(one_head, (jnp.swapaxes(queries, 0, 1), jnp.swapaxes(key_all, 0, 1), jnp.swapaxes(value_all, 0, 1)))
    attended = jnp.swapaxes(attended, 0, 1).reshape(TOKENS, HEADS * HEAD_DIM)
    hidden = (tokens.astype(jnp.float32) + jnp.dot(attended, w_out, preferred_element_type=jnp.float32)).astype(jnp.bfloat16)
    moe_in = rms_scale(hidden, moe_gain).astype(jnp.bfloat16)
    logits = jnp.dot(moe_in, w_router, preferred_element_type=jnp.float32)
    expert_range = jnp.arange(EXPERTS, dtype=jnp.int32)
    chosen = lax.optimization_barrier(jnp.sum(jnp.where(expert_ids[:, :, None] == expert_range[None, None, :], logits[:, None, :], 0.0), axis=2))
    gate_first = 1.0 / (1.0 + jnp.exp(chosen[:, 1] - chosen[:, 0]))
    gate_second = 1.0 / (1.0 + jnp.exp(chosen[:, 0] - chosen[:, 1]))
    gating = jnp.stack([gate_first, gate_second], axis=1)
    slot_of = lax.optimization_barrier(jnp.sum(jnp.where(old_place[:, None] == expert_range[None, :], expert_range[:, None], 0), axis=0, dtype=jnp.int32))
    slice_width = FF // N_SEQ
    capacity_rows = min(TOKENS, N_SEQ * N_EXP * CAP)

    def add_expert(moe_sum, expert):
        routed = jnp.any(expert_ids == expert, axis=1)
        found_rows = jnp.nonzero(routed, size=capacity_rows, fill_value=0)[0].astype(jnp.int32)
        valid_rows = jnp.arange(capacity_rows, dtype=jnp.int32) < jnp.sum(routed.astype(jnp.int32), dtype=jnp.int32)
        inputs = moe_in[found_rows]
        slot_index = slot_of[expert]
        gate_slices = jnp.moveaxis(gate_up[slot_index].reshape(2, D, N_SEQ, slice_width), 2, 0)
        down_slices = w_down[slot_index].reshape(N_SEQ, slice_width, D)

        def add_slice(running, operands):
            pair_weights, down_weights = operands
            gate_part = jnp.dot(inputs, pair_weights[0], preferred_element_type=jnp.float32)
            up_part = jnp.dot(inputs, pair_weights[1], preferred_element_type=jnp.float32)
            activated = (jax.nn.silu(gate_part) * up_part).astype(jnp.bfloat16)
            slice_term = jnp.dot(activated, down_weights, preferred_element_type=jnp.float32).astype(jnp.bfloat16)
            slice_term = lax.optimization_barrier(slice_term)
            return (running + slice_term.astype(jnp.float32), None)
        summed, _ = lax.scan(add_slice, jnp.zeros((capacity_rows, D), jnp.float32), (gate_slices, down_slices))
        expert_out = lax.optimization_barrier(summed.astype(jnp.bfloat16)).astype(jnp.float32)
        chosen_gate = lax.optimization_barrier(jnp.sum(jnp.where(expert_ids[found_rows] == expert, gating[found_rows], 0.0), axis=1))
        weighted = jnp.where(valid_rows[:, None], chosen_gate[:, None] * expert_out, 0.0)
        return (moe_sum.at[found_rows].add(weighted), None)
    moe_sum, _ = lax.scan(add_expert, jnp.zeros((TOKENS, D), jnp.float32), expert_range)
    layer_out = (hidden.astype(jnp.float32) + moe_sum).astype(jnp.bfloat16)
    source_slot = lax.optimization_barrier(jnp.sum(jnp.where(new_place[:, None] == expert_range[None, :], slot_of[None, :], 0), axis=1, dtype=jnp.int32))
    new_gate_up = gate_up[source_slot]
    new_down = w_down[source_slot]
    return (layer_out, new_gate_up, new_down)
```

```python
import jax
import jax.numpy as jnp
from jax import lax
from jax.sharding import Mesh, PartitionSpec as P

HEAD_DIM = 64
SEQ = ("zh", "x", "c")
EXP = ("zl", "y")

epsilon = 1e-05
masked_score = -1e30
F32 = jnp.float32
BF16 = jnp.bfloat16


def rms_scale(values_in, gain):
    widened = values_in.astype(F32)
    inverse = lax.rsqrt(jnp.mean(widened * widened, axis=-1, keepdims=True) + epsilon)
    return widened * inverse * gain.astype(F32)


def rotate(vectors, angle_base):
    halfway = vectors.shape[-1] // 2
    spacing = jnp.arange(halfway, dtype=F32) / halfway
    freqs_all = jnp.exp(-jnp.log(10000.0) * spacing)
    angles = angle_base[:, None] * freqs_all[None, :]
    cosine = jnp.cos(angles)[:, None, :]
    sine_part = jnp.sin(angles)[:, None, :]
    leading = vectors[..., :halfway]
    trailing = vectors[..., halfway:]
    return jnp.concatenate(
        [leading * cosine - trailing * sine_part, trailing * cosine + leading * sine_part], axis=-1
    )


def doc_layout(seq_lengths, row_ids):
    ending = jnp.cumsum(seq_lengths, dtype=jnp.int32)
    passed = (ending[None, :] <= row_ids[:, None]).astype(jnp.int32)
    starting = jnp.sum(passed * seq_lengths[None, :], axis=1, dtype=jnp.int32)
    return starting, row_ids - starting


def owner_table(placing):
    slot_range = jnp.arange(placing.shape[0], dtype=jnp.int32)
    return jnp.sum(
        jnp.where(placing[:, None] == slot_range[None, :], slot_range[:, None], 0),
        axis=0,
        dtype=jnp.int32,
    )


def shift(value, axis, by):
    count = lax.axis_size(axis)
    return lax.ppermute(value, axis, [(i, (i + by) % count) for i in range(count)])


def exchange(blocks, axis):
    count = lax.axis_size(axis)
    me = lax.axis_index(axis)
    received = []
    for step in range(count):
        target = (me + step) % count
        piece = lax.dynamic_index_in_dim(blocks, target, 0, keepdims=False)
        received.append(piece if step == 0 else shift(piece, axis, step))
    return received


def gather_near(value, axis):
    count = lax.axis_size(axis)
    return [value] + [shift(value, axis, step) for step in range(1, count)]


def by_index(pieces, axis):
    count = len(pieces)
    me = lax.axis_index(axis)
    stacked = jnp.stack(pieces)
    order = (me - jnp.arange(count, dtype=jnp.int32)) % count
    return jnp.take(stacked, order, axis=0)


def gather_experts(gate, down):
    gate_left, down_left = shift(gate, "x", 1), shift(down, "x", 1)
    gate_right, down_right = shift(gate, "x", -1), shift(down, "x", -1)
    cut = gate.shape[1] * 3 // 4
    far_low = shift(gate_left[:, :cut], "x", 1)
    far_high = shift(gate_right[:, cut:], "x", -1)
    far_down = shift(down_right, "x", -1)
    far_gate = jnp.concatenate([far_low, far_high], axis=1)
    mine = [(gate, down), (gate_left, down_left), (gate_right, down_right), (far_gate, far_down)]
    return mine + [(shift(g, "c", 1), shift(d, "c", 1)) for g, d in mine]


def run_experts(rows, pieces):
    total = None
    for gate, down in pieces:
        projected = lax.dot_general(
            rows, gate, (((1,), (2,)), ((), ())), preferred_element_type=F32
        )
        activated = (jax.nn.silu(projected[:, 0]) * projected[:, 1]).astype(BF16)
        part = jnp.dot(activated, down, preferred_element_type=F32)
        total = part if total is None else total + part
    return total


def attend(queries, query_rows, query_starts, keys, values, key_rows, seen):
    scores = jnp.dot(queries, keys.T, preferred_element_type=F32) * HEAD_DIM ** (-0.5)
    allowed = (
        (key_rows[None, :] >= query_starts[:, None])
        & (key_rows[None, :] <= query_rows[:, None])
        & seen
    )
    scores = jnp.where(allowed, scores, masked_score)
    largest = jnp.max(scores, axis=1, keepdims=True)
    weights = jnp.where(allowed, jnp.exp(scores - largest), 0.0)
    totals = jnp.sum(weights, axis=1, keepdims=True)
    summed = jnp.dot(weights.astype(BF16), values, preferred_element_type=F32)
    return (summed / totals).astype(BF16)


def shards(
    tokens,
    norm_gain,
    w_qkv,
    w_out,
    moe_gain,
    w_router,
    gate_up,
    w_down,
    lengths,
    blocks_seen,
    expert_ids,
    old_place,
    new_place,
):
    block_rows = tokens.shape[0]
    model_width = tokens.shape[1]
    exp_count = lax.axis_size(EXP)
    block_index = lax.axis_index(SEQ)
    slot_index = lax.axis_index(EXP)
    heads_here = w_qkv.shape[2] // HEAD_DIM
    slice_width = gate_up.shape[3]
    n_zh, n_x, n_c = lax.axis_size("zh"), lax.axis_size("x"), lax.axis_size("c")
    my_zh, my_x, my_c = lax.axis_index("zh"), lax.axis_index("x"), lax.axis_index("c")

    by_unit = jnp.transpose(gate_up[0], (2, 0, 1))
    gate_planes = jnp.transpose(by_unit, (1, 0, 2))
    down_rows = w_down[0]
    expert_pieces = gather_experts(gate_planes, down_rows)

    row_range = jnp.arange(block_rows, dtype=jnp.int32)
    my_starts, my_places = doc_layout(lengths, block_index * block_rows + row_range)
    normed = rms_scale(tokens, norm_gain).astype(BF16)
    projected = jnp.dot(
        normed,
        w_qkv.reshape(model_width, 3 * heads_here * HEAD_DIM),
        preferred_element_type=F32,
    ).reshape(block_rows, 3, heads_here, HEAD_DIM)
    angle_rows = my_places.astype(F32)
    queries = rotate(projected[:, 0], angle_rows).astype(BF16)
    keys = rotate(projected[:, 1], angle_rows).astype(BF16)
    values = projected[:, 2].astype(BF16)
    packed = jnp.concatenate([queries, keys, values], axis=-1)
    packed = jnp.transpose(packed, (1, 0, 2))

    by_head = exchange(packed, "zh")
    seen_near = gather_near(blocks_seen, "zh")
    queries_here = jnp.concatenate([piece[:, :HEAD_DIM] for piece in by_head], axis=0)
    pairs = jnp.concatenate([piece[:, HEAD_DIM:] for piece in by_head], axis=0)
    along_x = jnp.concatenate(gather_near(pairs, "x"), axis=0)
    pairs_all = jnp.concatenate([along_x, shift(along_x, "c", 1)], axis=0)

    dz = jnp.arange(n_zh, dtype=jnp.int32)
    near_zh = (my_zh - dz) % n_zh
    near_x = (my_x - jnp.arange(n_x, dtype=jnp.int32)) % n_x
    near_c = (my_c - jnp.arange(n_c, dtype=jnp.int32)) % n_c
    key_blocks = (
        near_zh[None, None, :] * (n_x * n_c) + near_x[None, :, None] * n_c + near_c[:, None, None]
    ).reshape(-1)
    key_rows = (key_blocks[:, None] * block_rows + row_range[None, :]).reshape(-1)
    query_blocks = near_zh * (n_x * n_c) + my_x * n_c + my_c
    query_rows = (query_blocks[:, None] * block_rows + row_range[None, :]).reshape(-1)
    query_starts, _ = doc_layout(lengths, query_rows)
    seen_rows = jnp.concatenate(seen_near, axis=0)
    block_range = jnp.arange(seen_rows.shape[1], dtype=jnp.int32)
    seen_near_first = jnp.sum(
        jnp.where(
            key_blocks[None, :, None] == block_range[None, None, :], seen_rows[:, None, :], 0
        ),
        axis=2,
    )
    seen_pairs = jnp.broadcast_to(
        (seen_near_first > 0)[:, None, :, None],
        (n_zh, block_rows, key_blocks.shape[0], block_rows),
    ).reshape(n_zh * block_rows, -1)
    attended = attend(
        queries_here,
        query_rows,
        query_starts,
        pairs_all[:, :HEAD_DIM],
        pairs_all[:, HEAD_DIM:],
        key_rows,
        seen_pairs,
    )

    attended = attended.reshape(n_zh, block_rows, HEAD_DIM)
    returned_heads = [attended[0]] + [shift(attended[step], "zh", -step) for step in range(1, n_zh)]
    stacked = jnp.stack(returned_heads)
    order = (jnp.arange(n_zh, dtype=jnp.int32) - my_zh) % n_zh
    heads_first = jnp.take(stacked, order, axis=0)
    attended = jnp.transpose(heads_first, (1, 0, 2)).reshape(block_rows, heads_here * HEAD_DIM)

    shard_rows = block_rows // exp_count
    partial = jnp.dot(attended, w_out, preferred_element_type=F32).astype(BF16)
    partial = lax.all_to_all(
        partial.reshape(exp_count, shard_rows, model_width), EXP, 0, 0, tiled=True
    )
    head_total = jnp.sum(partial.astype(F32), axis=0)
    residual = lax.dynamic_slice_in_dim(tokens, slot_index * shard_rows, shard_rows, 0)
    hidden = (residual.astype(F32) + head_total).astype(BF16)
    moe_in = rms_scale(hidden, moe_gain).astype(BF16)
    logits = jnp.dot(moe_in, w_router, preferred_element_type=F32)
    expert_count = w_router.shape[1]
    expert_range = jnp.arange(expert_count, dtype=jnp.int32)
    chosen = jnp.sum(
        jnp.where(expert_ids[:, :, None] == expert_range[None, None, :], logits[:, None, :], 0.0),
        axis=2,
    )
    gate_first = 1.0 / (1.0 + jnp.exp(chosen[:, 1] - chosen[:, 0]))
    gate_second = 1.0 / (1.0 + jnp.exp(chosen[:, 0] - chosen[:, 1]))
    gating = jnp.stack([gate_first, gate_second], axis=1)

    slot_old = owner_table(old_place)
    capacity = min(shard_rows, 4 * shard_rows // exp_count)
    slot_total = exp_count * capacity
    pair_ids = expert_ids.reshape(-1)
    pair_marks = (pair_ids[:, None] == expert_range[None, :]).astype(jnp.int32)
    earlier = jnp.cumsum(pair_marks, axis=0, dtype=jnp.int32) - pair_marks
    rank_in = jnp.sum(earlier * pair_marks, axis=1, dtype=jnp.int32)
    owner_of = jnp.sum(pair_marks * slot_old[None, :], axis=1, dtype=jnp.int32)
    target = (owner_of * capacity + rank_in).reshape(shard_rows, 2)
    slot_range = jnp.arange(slot_total, dtype=jnp.int32)
    marks = target[:, :, None] == slot_range[None, None, :]
    selector = jnp.any(marks, axis=1)
    outgoing = lax.dot_general(
        selector.astype(BF16), moe_in, (((0,), (0,)), ((), ())), preferred_element_type=F32
    )
    outgoing = outgoing.astype(BF16).reshape(exp_count, capacity, model_width)
    arrived = lax.all_to_all(outgoing, EXP, 0, 0, tiled=True).reshape(slot_total, model_width)
    rows_near = jnp.concatenate(gather_near(arrived, "zh"), axis=0)
    parts = run_experts(rows_near, expert_pieces).astype(BF16)
    parts = parts.reshape(n_zh, slot_total, model_width)
    summed = parts[0].astype(F32)
    for step in range(1, n_zh):
        summed = summed + shift(parts[step], "zh", -step).astype(F32)
    summed = summed.astype(BF16).reshape(exp_count, capacity, model_width)
    returned = lax.all_to_all(summed, EXP, 0, 0, tiled=True)
    spread = jnp.sum(jnp.where(marks, gating[:, :, None], 0.0), axis=1)
    moe_sum = jnp.dot(
        spread,
        returned.reshape(slot_total, model_width).astype(F32),
        precision=lax.Precision.HIGHEST,
    )
    layer_out = (hidden.astype(F32) + moe_sum).astype(BF16)

    source_slot = jnp.sum(
        jnp.where(new_place[:, None] == expert_range[None, :], slot_old[None, :], 0),
        axis=1,
        dtype=jnp.int32,
    )

    def move(array, piece):
        spare = exp_count * piece - array.shape[0]
        padded = jnp.pad(array, ((0, spare),) + ((0, 0),) * (array.ndim - 1))
        split = padded.reshape((exp_count, piece) + array.shape[1:])
        held = lax.all_to_all(split, EXP, 0, 0, tiled=True)
        ordered = jnp.take(held, source_slot, axis=0)
        moved = lax.all_to_all(ordered, EXP, 0, 0, tiled=True)
        return moved.reshape((exp_count * piece,) + array.shape[1:])[: array.shape[0]]

    gate_piece = -(-slice_width // exp_count)
    down_piece = -(-slice_width // (8 * exp_count)) * 8
    new_gate_up = jnp.transpose(move(by_unit, gate_piece), (1, 2, 0))[None]
    new_down = move(down_rows, down_piece)[None]
    return (layer_out, new_gate_up, new_down)


def solution(mesh):
    fine = Mesh(mesh.devices.reshape(4, 4, 2, 2, 4), SEQ + EXP)
    in_specs = (
        P(SEQ, None),
        P(),
        P(None, None, EXP),
        P(EXP, None),
        P(),
        P(),
        P(EXP, None, None, SEQ),
        P(EXP, SEQ, None),
        P(),
        P(SEQ, None),
        P(SEQ + EXP, None),
        P(),
        P(),
    )
    out_specs = (P(SEQ + EXP, None), P(EXP, None, None, SEQ), P(EXP, SEQ, None))
    return jax.shard_map(shards, mesh=fine, in_specs=in_specs, out_specs=out_specs, check_vma=False)
```

```python
import functools

import jax
import jax.numpy as jnp
from jax import lax
from jax.experimental import pallas as pl
from jax.experimental.pallas import tpu as pltpu
from jax.sharding import Mesh, PartitionSpec as P

HEAD_DIM = 64
SEQ = ("zh", "x", "c")
EXP = ("zl", "y")

epsilon = 1e-05
masked_score = -1e30
F32 = jnp.float32
BF16 = jnp.bfloat16
I32 = jnp.int32


def rms_scale(values_in, gain):
    widened = values_in.astype(F32)
    inverse = lax.rsqrt(jnp.mean(widened * widened, axis=-1, keepdims=True) + epsilon)
    return widened * inverse * gain.astype(F32)


def rotate(vectors, angle_base):
    halfway = vectors.shape[-1] // 2
    spacing = jnp.arange(halfway, dtype=F32) / halfway
    freqs_all = jnp.exp(-jnp.log(10000.0) * spacing)
    angles = angle_base[:, None] * freqs_all[None, :]
    cosine = jnp.cos(angles)[:, None, :]
    sine_part = jnp.sin(angles)[:, None, :]
    leading = vectors[..., :halfway]
    trailing = vectors[..., halfway:]
    return jnp.concatenate(
        [leading * cosine - trailing * sine_part, trailing * cosine + leading * sine_part], axis=-1
    )


def row_places(seq_lengths, row_ids):
    ending = jnp.cumsum(seq_lengths, dtype=I32)
    passed = (ending[None, :] <= row_ids[:, None]).astype(I32)
    starting = jnp.sum(passed * seq_lengths[None, :], axis=1, dtype=I32)
    return row_ids - starting


def owner_table(placing):
    slot_range = jnp.arange(placing.shape[0], dtype=I32)
    return jnp.sum(
        jnp.where(placing[:, None] == slot_range[None, :], slot_range[:, None], 0),
        axis=0,
        dtype=I32,
    )


def shift(value, axis, by):
    count = lax.axis_size(axis)
    return lax.ppermute(value, axis, [(i, (i + by) % count) for i in range(count)])


def gather_near(value, axis):
    return [value] + [shift(value, axis, step) for step in range(1, lax.axis_size(axis))]


def tie(*values):
    return lax.optimization_barrier(values)


def attend_kernel(n_x, n_c, where_ref, lengths_ref, q_ref, near_ref, other_ref, out_ref, largest, totals, summed):
    n_zh, rows, _ = q_ref.shape
    my_zh, my_x, my_c = where_ref[0], where_ref[1], where_ref[2]
    n_docs = lengths_ref.shape[0]
    lane = lax.broadcasted_iota(I32, (rows, 128), 1)
    column = lax.broadcasted_iota(I32, (1, rows), 1)
    row_iota = lax.broadcasted_iota(I32, (rows, 1), 0)

    def one_query_block(dq, _):
        zh_q = lax.rem(my_zh - dq + n_zh, n_zh)
        row_ids = (zh_q * (n_x * n_c) + my_x * n_c + my_c) * rows + row_iota
        starts = jnp.zeros((rows, 1), I32)
        ending = 0
        for doc in range(n_docs):
            ending = ending + lengths_ref[doc]
            starts = jnp.where(row_ids >= ending, ending, starts)
        queries = q_ref[dq]
        largest[...] = jnp.full(largest.shape, masked_score, F32)
        totals[...] = jnp.zeros(totals.shape, F32)
        summed[...] = jnp.zeros(summed.shape, F32)

        def one_quarter(dz, _):
            zh_k = lax.rem(my_zh - dz + n_zh, n_zh)

            @pl.when(zh_k <= zh_q)
            def _():
                keys, values, key_ids = [], [], []
                for dc in range(n_c):
                    source = near_ref if dc == 0 else other_ref
                    at_c = lax.rem(my_c - dc + n_c, n_c)
                    for dx in range(n_x):
                        at_x = lax.rem(my_x - dx + n_x, n_x)
                        block = zh_k * (n_x * n_c) + at_x * n_c + at_c
                        first = pl.multiple_of(dx * (n_zh * rows) + dz * rows, rows)
                        pair = source[pl.ds(first, rows), :]
                        values.append(pair)
                        mark = jnp.where(lane == block + HEAD_DIM, 1.0, 0.0).astype(BF16)
                        keys.append(jnp.where(lane < HEAD_DIM, pair, mark))
                        key_ids.append(block * rows + column)
                keys = jnp.concatenate(keys, axis=0)
                values = jnp.concatenate(values, axis=0)
                key_ids = jnp.concatenate(key_ids, axis=1)
                scores = lax.dot_general(
                    queries, keys, (((1,), (1,)), ((), ())), preferred_element_type=F32
                )
                allowed = (key_ids >= starts) & (key_ids <= row_ids)
                scores = jnp.where(allowed, scores, masked_score)
                old = largest[:, :1]
                new = jnp.maximum(old, jnp.max(scores, axis=1, keepdims=True))
                weights = jnp.where(allowed, jnp.exp(scores - new), 0.0)
                fade = jnp.exp(old - new)
                totals[...] = totals[...] * fade + jnp.sum(weights, axis=1, keepdims=True)
                summed[...] = summed[...] * fade + jnp.dot(
                    weights.astype(BF16), values, preferred_element_type=F32
                )
                largest[...] = jnp.broadcast_to(new, largest.shape)

            return 0

        lax.fori_loop(0, n_zh, one_quarter, 0)
        mixed = summed[...] / totals[...]
        out_ref[dq] = mixed[:, HEAD_DIM:].astype(BF16)
        return 0

    lax.fori_loop(0, n_zh, one_query_block, 0)


def attend(where, lengths, queries, near, other, n_x, n_c):
    n_zh, rows, _ = queries.shape
    vmem = pl.BlockSpec(memory_space=pltpu.VMEM)
    smem = pl.BlockSpec(memory_space=pltpu.SMEM)
    keys = near.shape[0] * 2
    return pl.pallas_call(
        functools.partial(attend_kernel, n_x, n_c),
        out_shape=jax.ShapeDtypeStruct((n_zh, rows, HEAD_DIM), BF16),
        in_specs=[smem, smem, vmem, vmem, vmem],
        out_specs=vmem,
        scratch_shapes=[pltpu.VMEM((rows, 128), F32)] * 3,
        compiler_params=pltpu.CompilerParams(vmem_limit_bytes=24 << 20),
        cost_estimate=pl.CostEstimate(
            flops=4 * n_zh * rows * keys * 128, bytes_accessed=2 << 20, transcendentals=n_zh * rows * keys
        ),
        name="attend",
    )(where, lengths, queries, near, other)


def experts_kernel(count, *refs):
    rows_ref = refs[0]
    gates, downs = refs[1 : 1 + count], refs[1 + count : 1 + 2 * count]
    out_ref, gate_held, down_held, total, gate_sem, down_sem = refs[1 + 2 * count :]
    for i in range(count):
        pltpu.make_async_copy(gates[i], gate_held.at[i], gate_sem.at[i]).start()
        pltpu.make_async_copy(downs[i], down_held.at[i], down_sem.at[i]).start()
    total[...] = jnp.zeros(total.shape, F32)

    def one_slice(i, _):
        pltpu.make_async_copy(gates[0], gate_held.at[i], gate_sem.at[i]).wait()
        rows = rows_ref[...]
        across = (((1,), (1,)), ((), ()))
        gate = lax.dot_general(rows, gate_held[i, 0], across, preferred_element_type=F32)
        up = lax.dot_general(rows, gate_held[i, 1], across, preferred_element_type=F32)
        activated = (gate / (1.0 + jnp.exp(-gate)) * up).astype(BF16)
        pltpu.make_async_copy(downs[0], down_held.at[i], down_sem.at[i]).wait()
        total[...] += jnp.dot(activated, down_held[i], preferred_element_type=F32)
        return 0

    lax.fori_loop(0, count, one_slice, 0)
    out_ref[...] = total[...].astype(BF16)


def run_experts(rows, pieces):
    count = len(pieces)
    width = rows.shape[1]
    units = pieces[0][1].shape[0]
    vmem = pl.BlockSpec(memory_space=pltpu.VMEM)
    anywhere = pl.BlockSpec(memory_space=pl.ANY)
    gates, downs = [g for g, _ in pieces], [d for _, d in pieces]
    return pl.pallas_call(
        functools.partial(experts_kernel, count),
        out_shape=jax.ShapeDtypeStruct(rows.shape, BF16),
        in_specs=[vmem] + [anywhere] * (2 * count),
        out_specs=vmem,
        scratch_shapes=[
            pltpu.VMEM((count, 2, units, width), BF16),
            pltpu.VMEM((count, units, width), BF16),
            pltpu.VMEM(rows.shape, F32),
            pltpu.SemaphoreType.DMA((count,)),
            pltpu.SemaphoreType.DMA((count,)),
        ],
        compiler_params=pltpu.CompilerParams(vmem_limit_bytes=48 << 20),
        cost_estimate=pl.CostEstimate(
            flops=6 * rows.shape[0] * width * units * count,
            bytes_accessed=6 * width * units * count,
            transcendentals=rows.shape[0] * units * count,
        ),
        name="experts",
    )(rows, *gates, *downs)


def shards(
    tokens,
    norm_gain,
    w_qkv,
    w_out,
    moe_gain,
    w_router,
    gate_up,
    w_down,
    lengths,
    blocks_seen,
    expert_ids,
    old_place,
    new_place,
):
    block_rows = tokens.shape[0]
    model_width = tokens.shape[1]
    exp_count = lax.axis_size(EXP)
    block_index = lax.axis_index(SEQ)
    slot_index = lax.axis_index(EXP)
    heads_here = w_qkv.shape[2] // HEAD_DIM
    slice_width = gate_up.shape[3]
    shard_rows = block_rows // exp_count
    n_zh, n_x, n_c = lax.axis_size("zh"), lax.axis_size("x"), lax.axis_size("c")
    my_zh, my_x, my_c = lax.axis_index("zh"), lax.axis_index("x"), lax.axis_index("c")
    expert_count = w_router.shape[1]
    expert_range = jnp.arange(expert_count, dtype=I32)

    by_unit = jnp.transpose(gate_up[0], (2, 0, 1))
    gate = jnp.transpose(by_unit, (1, 0, 2))
    down = w_down[0]
    down_left, down_right = shift(down, "x", 1), shift(down, "x", -1)
    gate_left, gate_right = shift(gate, "x", 1), shift(gate, "x", -1)

    slot_old = owner_table(old_place)
    source_slot = jnp.sum(
        jnp.where(new_place[:, None] == expert_range[None, :], slot_old[None, :], 0),
        axis=1,
        dtype=I32,
    )

    def split(array, piece):
        spare = exp_count * piece - array.shape[0]
        padded = jnp.pad(array, ((0, spare),) + ((0, 0),) * (array.ndim - 1))
        return padded.reshape((exp_count, piece) + array.shape[1:])

    def spread_pieces(array, piece):
        return lax.all_to_all(split(array, piece), EXP, 0, 0, tiled=True)

    gate_spread = spread_pieces(by_unit, -(-slice_width // exp_count))
    down_spread = spread_pieces(down, -(-slice_width // (8 * exp_count)) * 8)

    row_range = jnp.arange(block_rows, dtype=I32)
    my_places = row_places(lengths, block_index * block_rows + row_range)
    normed = rms_scale(tokens, norm_gain).astype(BF16)
    q_out, k_out, v_out = (
        jnp.dot(normed, w_qkv[:, i], preferred_element_type=F32).reshape(
            block_rows, heads_here, HEAD_DIM
        )
        for i in range(3)
    )
    angle_rows = my_places.astype(F32)
    queries = rotate(q_out, angle_rows).astype(BF16) * BF16(HEAD_DIM ** (-0.5))
    keys = rotate(k_out, angle_rows).astype(BF16)
    values = v_out.astype(BF16)
    unseen = jnp.where(blocks_seen > 0, 0.0, masked_score).astype(BF16)
    unseen = jnp.broadcast_to(unseen, (block_rows, unseen.shape[1]))
    ids_lanes = jnp.pad(
        expert_ids.astype(BF16),
        ((0, block_rows - shard_rows), (0, HEAD_DIM - unseen.shape[1] - 2)),
    )
    extra = jnp.concatenate([unseen, ids_lanes], axis=1)
    packed = jnp.stack(
        [
            jnp.concatenate([queries[:, h], extra, keys[:, h], values[:, h]], axis=1)
            for h in range(heads_here)
        ]
    )

    by_head = []
    for step in range(n_zh):
        piece = lax.dynamic_index_in_dim(packed, (my_zh + step) % n_zh, 0, keepdims=False)
        by_head.append(piece if step == 0 else shift(piece, "zh", step))
    queries_here = jnp.stack([piece[:, :128] for piece in by_head])
    pairs = jnp.concatenate([piece[:, 128:] for piece in by_head], axis=0)
    near = jnp.concatenate(gather_near(pairs, "x"), axis=0)
    other = shift(near, "c", 1)
    where = jnp.stack([my_zh, my_x, my_c]).astype(I32)
    attended = attend(where, lengths, queries_here, near, other, n_x, n_c)

    returned = [attended[0]] + [shift(attended[step], "zh", -step) for step in range(1, n_zh)]
    order = (my_zh + jnp.arange(n_zh, dtype=I32)) % n_zh
    w_out_near = jnp.take(w_out.reshape(n_zh, HEAD_DIM, model_width), order, axis=0)
    w_out_near = w_out_near.reshape(w_out.shape)
    attended = jnp.concatenate(returned, axis=1)
    partial = jnp.dot(attended, w_out_near, preferred_element_type=F32).astype(BF16)
    partial = partial.reshape(exp_count, shard_rows, model_width)

    partial, gate_left, gate_right, down_left, down_right = tie(
        partial, gate_left, gate_right, down_left, down_right
    )
    cut = slice_width * 3 // 4
    far_low = shift(gate_left[:, :cut], "x", 1)
    far_high = shift(gate_right[:, cut:], "x", -1)
    far_down = shift(down_right, "x", -1)
    pieces = [(gate, down), (gate_left, down_left), (gate_right, down_right)]
    pieces_other = [(shift(g, "c", 1), shift(d, "c", 1)) for g, d in pieces]

    partial = lax.all_to_all(partial, EXP, 0, 0, tiled=True)
    head_total = jnp.sum(partial.astype(F32), axis=0)
    residual = lax.dynamic_slice_in_dim(tokens, slot_index * shard_rows, shard_rows, 0)
    hidden = (residual.astype(F32) + head_total).astype(BF16)
    moe_in = rms_scale(hidden, moe_gain).astype(BF16)

    rows_near = jnp.concatenate(gather_near(moe_in, "zh"), axis=0)
    ids_near = jnp.concatenate(
        [q[:shard_rows, 96:98] for q in queries_here], axis=0
    ).astype(F32).astype(I32)
    capacity = min(shard_rows, 4 * shard_rows // exp_count)
    near_rows = n_zh * shard_rows
    pair_ids = ids_near.reshape(n_zh, 2 * shard_rows)
    pair_marks = (pair_ids[:, :, None] == expert_range[None, None, :]).astype(I32)
    earlier = jnp.cumsum(pair_marks, axis=1, dtype=I32) - pair_marks
    rank_in = jnp.sum(earlier * pair_marks, axis=2, dtype=I32)
    owner_of = jnp.sum(pair_marks * slot_old[None, None, :], axis=2, dtype=I32)
    target = (owner_of * n_zh + jnp.arange(n_zh, dtype=I32)[:, None]) * capacity + rank_in
    target = target.reshape(near_rows, 2)
    slot_range = jnp.arange(exp_count * n_zh * capacity, dtype=I32)
    marks = target[:, :, None] == slot_range[None, None, :]
    selector = jnp.any(marks, axis=1).astype(BF16)
    outgoing = lax.dot_general(
        selector, rows_near, (((0,), (0,)), ((), ())), preferred_element_type=F32
    ).astype(BF16)
    arrived = lax.all_to_all(
        outgoing.reshape(exp_count, n_zh * capacity, model_width), EXP, 0, 0, tiled=True
    ).reshape(-1, model_width)

    logits = jnp.dot(rows_near, w_router, preferred_element_type=F32)
    chosen = jnp.sum(
        jnp.where(ids_near[:, :, None] == expert_range[None, None, :], logits[:, None, :], 0.0),
        axis=2,
    )
    gate_first = 1.0 / (1.0 + jnp.exp(chosen[:, 1] - chosen[:, 0]))
    gate_second = 1.0 / (1.0 + jnp.exp(chosen[:, 0] - chosen[:, 1]))
    gating = jnp.stack([gate_first, gate_second], axis=1)
    spread = jnp.sum(jnp.where(marks, gating[:, :, None], 0.0), axis=1)

    far_gate = jnp.concatenate([far_low, far_high], axis=1)
    pieces.append((far_gate, far_down))
    pieces_other.append((shift(far_gate, "c", 1), shift(far_down, "c", 1)))
    parts = run_experts(arrived, pieces + pieces_other)
    back = lax.all_to_all(
        parts.reshape(exp_count, n_zh * capacity, model_width), EXP, 0, 0, tiled=True
    ).reshape(-1, model_width)
    combined = jnp.dot(spread, back.astype(F32), precision=lax.Precision.HIGHEST)
    combined = combined.astype(BF16).reshape(n_zh, shard_rows, model_width)
    moe_sum = combined[0].astype(F32)
    for step in range(1, n_zh):
        moe_sum = moe_sum + shift(combined[step], "zh", -step).astype(F32)
    layer_out = (hidden.astype(F32) + moe_sum).astype(BF16)

    def settle(held, units):
        ordered = jnp.take(held, source_slot, axis=0)
        moved = lax.all_to_all(ordered, EXP, 0, 0, tiled=True)
        return moved.reshape((-1,) + held.shape[2:])[:units]

    new_gate_up = jnp.transpose(settle(gate_spread, slice_width), (1, 2, 0))[None]
    new_down = settle(down_spread, slice_width)[None]
    return (layer_out, new_gate_up, new_down)


def solution(mesh):
    fine = Mesh(mesh.devices.reshape(4, 4, 2, 2, 4), SEQ + EXP)
    in_specs = (
        P(SEQ, None),
        P(),
        P(None, None, EXP),
        P(EXP, None),
        P(),
        P(),
        P(EXP, None, None, SEQ),
        P(EXP, SEQ, None),
        P(),
        P(SEQ, None),
        P(SEQ + EXP, None),
        P(),
        P(),
    )
    out_specs = (P(SEQ + EXP, None), P(EXP, None, None, SEQ), P(EXP, SEQ, None))
    return jax.shard_map(shards, mesh=fine, in_specs=in_specs, out_specs=out_specs, check_vma=False)
```

```python
import functools

import jax
import jax.numpy as jnp
from jax import lax
from jax.experimental import pallas as pl
from jax.experimental.pallas import tpu as pltpu
from jax.sharding import Mesh, PartitionSpec as P

HEAD_DIM = 64
SEQ = ("zh", "x", "c")
EXP = ("zl", "y")

epsilon = 1e-05
masked_score = -1e30
F32 = jnp.float32
BF16 = jnp.bfloat16
I32 = jnp.int32


def rms_scale(values_in, gain):
    widened = values_in.astype(F32)
    inverse = lax.rsqrt(jnp.mean(widened * widened, axis=-1, keepdims=True) + epsilon)
    return widened * inverse * gain.astype(F32)


def row_places(seq_lengths, row_ids):
    ending = jnp.cumsum(seq_lengths, dtype=I32)
    passed = (ending[None, :] <= row_ids[:, None]).astype(I32)
    starting = jnp.sum(passed * seq_lengths[None, :], axis=1, dtype=I32)
    return row_ids - starting


def owner_table(placing):
    slot_range = jnp.arange(placing.shape[0], dtype=I32)
    return jnp.sum(
        jnp.where(placing[:, None] == slot_range[None, :], slot_range[:, None], 0),
        axis=0,
        dtype=I32,
    )


def shift(value, axis, by):
    count = lax.axis_size(axis)
    return lax.ppermute(value, axis, [(i, (i + by) % count) for i in range(count)])


def gather_near(value, axis):
    return [value] + [shift(value, axis, step) for step in range(1, lax.axis_size(axis))]


def tie(*values):
    return lax.optimization_barrier(values)


def attend_kernel(n_x, n_c, where_ref, lengths_ref, queries_ref, near_ref, other_ref, out_ref, held):
    n_zh, rows, _ = out_ref.shape
    my_zh, my_x, my_c = where_ref[0], where_ref[1], where_ref[2]
    lane = lax.broadcasted_iota(I32, (rows, 128), 1)
    column = lax.broadcasted_iota(I32, (1, rows), 1)
    row_iota = lax.broadcasted_iota(I32, (rows, 1), 0)

    def pair_of(dz, dc, dx):
        source = near_ref if dc == 0 else other_ref
        first = pl.multiple_of(dx * (n_zh * rows) + dz * rows, rows)
        return source[pl.ds(first, rows), :]

    for dq in range(n_zh):
        zh_q = lax.rem(my_zh - dq + n_zh, n_zh)
        row_ids = (zh_q * (n_x * n_c) + my_x * n_c + my_c) * rows + row_iota
        starts = jnp.zeros((rows, 1), I32)
        ending = 0
        for doc in range(lengths_ref.shape[0]):
            ending = ending + lengths_ref[doc]
            starts = jnp.where(row_ids >= ending, ending, starts)
        queries = queries_ref[dq * rows : (dq + 1) * rows, :]

        def score(dz, largest):
            zh_k = lax.rem(my_zh - dz + n_zh, n_zh)

            def run(largest):
                for dc in range(n_c):
                    at_c = lax.rem(my_c - dc + n_c, n_c)
                    for dx in range(n_x):
                        at_x = lax.rem(my_x - dx + n_x, n_x)
                        block = zh_k * (n_x * n_c) + at_x * n_c + at_c
                        mark = jnp.where(lane == block + HEAD_DIM, 1.0, 0.0).astype(BF16)
                        keys = jnp.where(lane < HEAD_DIM, pair_of(dz, dc, dx), mark)
                        scores = lax.dot_general(
                            queries, keys, (((1,), (1,)), ((), ())), preferred_element_type=F32
                        )
                        key_ids = block * rows + column
                        allowed = (key_ids >= starts) & (key_ids <= row_ids)
                        scores = jnp.where(allowed, scores, masked_score)
                        held[dz, dc * n_x + dx] = scores
                        largest = jnp.maximum(largest, scores)
                return largest

            return lax.cond(zh_k <= zh_q, run, lambda v: v, largest)

        largest = lax.fori_loop(
            0, n_zh, score, jnp.full((rows, 128), masked_score, F32)
        )
        top = jnp.max(largest, axis=1, keepdims=True)

        def mix(dz, state):
            zh_k = lax.rem(my_zh - dz + n_zh, n_zh)

            def run(state):
                totals, summed = state
                for dc in range(n_c):
                    for dx in range(n_x):
                        weights = jnp.exp(held[dz, dc * n_x + dx] - top)
                        totals = totals + weights
                        summed = summed + jnp.dot(
                            weights.astype(BF16), pair_of(dz, dc, dx), preferred_element_type=F32
                        )
                return totals, summed

            return lax.cond(zh_k <= zh_q, run, lambda v: v, state)

        nothing = jnp.zeros((rows, 128), F32)
        totals, summed = lax.fori_loop(0, n_zh, mix, (nothing, nothing))
        mixed = summed / jnp.sum(totals, axis=1, keepdims=True)
        out_ref[dq] = mixed[:, HEAD_DIM:].astype(BF16)


def attend(where, lengths, queries, near, other, n_zh, n_x, n_c):
    rows = queries.shape[0] // n_zh
    vmem = pl.BlockSpec(memory_space=pltpu.VMEM)
    smem = pl.BlockSpec(memory_space=pltpu.SMEM)
    keys = near.shape[0] * 2
    return pl.pallas_call(
        functools.partial(attend_kernel, n_x, n_c),
        out_shape=jax.ShapeDtypeStruct((n_zh, rows, HEAD_DIM), BF16),
        in_specs=[smem, smem, vmem, vmem, vmem],
        out_specs=vmem,
        scratch_shapes=[pltpu.VMEM((n_zh, n_c * n_x, rows, 128), F32)],
        compiler_params=pltpu.CompilerParams(vmem_limit_bytes=24 << 20),
        cost_estimate=pl.CostEstimate(
            flops=4 * n_zh * rows * keys * 128, bytes_accessed=2 << 20, transcendentals=n_zh * rows * keys
        ),
        name="attend",
    )(where, lengths, queries, near, other)


def project_kernel(where_ref, tokens_ref, gain_ref, weight_ref, cos_ref, sin_ref, extra_ref, *refs):
    outs, held = refs[:-1], refs[-1]
    widened = tokens_ref[...].astype(F32)
    inverse = lax.rsqrt(jnp.mean(widened * widened, axis=-1, keepdims=True) + epsilon)
    normed = (widened * inverse * gain_ref[...].astype(F32)).astype(BF16)
    q, k, v = (
        jnp.dot(normed, weight_ref[i], preferred_element_type=F32) for i in range(3)
    )
    rows, width = q.shape
    cosine = jnp.concatenate([cos_ref[...]] * (width // 128), axis=1)
    sine = jnp.concatenate([sin_ref[...]] * (width // 128), axis=1)
    lane = lax.broadcasted_iota(I32, (rows, width), 1)
    first_half = lax.rem(lane, HEAD_DIM) < HEAD_DIM // 2
    low = lax.broadcasted_iota(I32, (rows, 128), 1) < HEAD_DIM

    def rotated(value):
        ahead = pltpu.roll(value, width - HEAD_DIM // 2, 1)
        behind = pltpu.roll(value, HEAD_DIM // 2, 1)
        return value * cosine + jnp.where(first_half, ahead, behind) * sine

    q, k = rotated(q) * HEAD_DIM ** (-0.5), rotated(k)
    heads = len(outs)
    for head in range(heads):
        columns = slice(head // 2 * 128, head // 2 * 128 + 128)
        q_here, k_here, v_here = q[:, columns], k[:, columns], v[:, columns]
        if head % 2:
            q_here, k_here = pltpu.roll(q_here, HEAD_DIM, 1), pltpu.roll(k_here, HEAD_DIM, 1)
        else:
            v_here = pltpu.roll(v_here, HEAD_DIM, 1)
        held[head, :, :128] = jnp.where(low, q_here, extra_ref[...]).astype(BF16)
        held[head, :, 128:] = jnp.where(low, k_here, v_here).astype(BF16)
    for step in range(heads):
        outs[step][...] = held[lax.rem(where_ref[0] + step, heads)]


def project(where, tokens, gain, weight, cosine, sine, extra):
    rows, width = tokens.shape
    heads = weight.shape[2] // HEAD_DIM
    vmem = pl.BlockSpec(memory_space=pltpu.VMEM)
    packet = jax.ShapeDtypeStruct((rows, 256), BF16)
    return pl.pallas_call(
        project_kernel,
        out_shape=[packet] * heads,
        in_specs=[pl.BlockSpec(memory_space=pltpu.SMEM)] + [vmem] * 6,
        out_specs=[vmem] * heads,
        scratch_shapes=[pltpu.VMEM((heads, rows, 256), BF16)],
        compiler_params=pltpu.CompilerParams(vmem_limit_bytes=24 << 20),
        cost_estimate=pl.CostEstimate(
            flops=6 * rows * width * heads * HEAD_DIM,
            bytes_accessed=2 * weight.size + 2 * tokens.size,
            transcendentals=0,
        ),
        name="project",
    )(where, tokens, gain[None], weight, cosine, sine, extra)


def join_kernel(*refs):
    pairs_ref, queries_ref, ids_ref = refs[-3:]
    count = len(refs) - 3
    rows, few = refs[0].shape[0], ids_ref.shape[0] // count
    for i, ref in enumerate(refs[:-3]):
        pairs_ref[i * rows : (i + 1) * rows, :] = ref[:, 128:]
        queries_ref[i * rows : (i + 1) * rows, :] = ref[:, :128]
        ids_ref[i * few : (i + 1) * few, :] = ref[:few, :128]


def join_packets(packets, few):
    rows, count = packets[0].shape[0], len(packets)
    vmem = pl.BlockSpec(memory_space=pltpu.VMEM)
    return pl.pallas_call(
        join_kernel,
        out_shape=[
            jax.ShapeDtypeStruct((count * rows, 128), BF16),
            jax.ShapeDtypeStruct((count * rows, 128), BF16),
            jax.ShapeDtypeStruct((count * few, 128), BF16),
        ],
        in_specs=[vmem] * count,
        out_specs=[vmem] * 3,
        name="join",
    )(*packets)


def output_kernel(where_ref, weight_ref, *refs):
    out_ref = refs[-1]
    heads = len(refs) - 1
    total = None
    for step in range(heads):
        head = lax.rem(where_ref[0] + step, heads)
        weight = weight_ref[pl.ds(pl.multiple_of(head * HEAD_DIM, HEAD_DIM), HEAD_DIM), :]
        part = jnp.dot(refs[step][...], weight, preferred_element_type=F32)
        total = part if total is None else total + part
    out_ref[...] = total.astype(BF16)


def output_projection(where, weight, returned):
    rows = returned[0].shape[0]
    vmem = pl.BlockSpec(memory_space=pltpu.VMEM)
    return pl.pallas_call(
        output_kernel,
        out_shape=jax.ShapeDtypeStruct((rows, weight.shape[1]), BF16),
        in_specs=[pl.BlockSpec(memory_space=pltpu.SMEM)] + [vmem] * (1 + len(returned)),
        out_specs=vmem,
        compiler_params=pltpu.CompilerParams(vmem_limit_bytes=16 << 20),
        cost_estimate=pl.CostEstimate(
            flops=2 * rows * weight.size, bytes_accessed=2 * weight.size, transcendentals=0
        ),
        name="output",
    )(where, weight, *returned)


def reorder_kernel(order_ref, held_ref, out_ref):
    out_ref[...] = held_ref[...]


def reorder(order, held):
    block = (1,) + held.shape[1:]
    rest = (0,) * (held.ndim - 1)
    return pl.pallas_call(
        reorder_kernel,
        out_shape=jax.ShapeDtypeStruct(held.shape, held.dtype),
        grid_spec=pltpu.PrefetchScalarGridSpec(
            num_scalar_prefetch=1,
            grid=(held.shape[0],),
            in_specs=[pl.BlockSpec(block, lambda i, order: (order[i],) + rest)],
            out_specs=pl.BlockSpec(block, lambda i, order: (i,) + rest),
        ),
        cost_estimate=pl.CostEstimate(flops=0, bytes_accessed=4 * held.size, transcendentals=0),
        name="reorder",
    )(order, held)


def experts_kernel(units, parts, *refs):
    rows_ref = refs[0]
    pieces, count = refs[1 : 1 + sum(parts)], len(parts)
    out_ref, held, mixed, acts, sems = refs[1 + len(pieces) :]
    width = held.shape[3]
    copies, used = [], 0
    for i in range(count):
        first = 0
        for ref in pieces[used : used + parts[i]]:
            last = first + ref.shape[0]
            copies.append(pltpu.make_async_copy(ref, held.at[i, first:last], sems.at[len(copies)]))
            first = last
        used += parts[i]
    for copy in copies:
        copy.start()
    used = 0
    for i in range(count):
        for copy in copies[used : used + parts[i]]:
            copy.wait()
        used += parts[i]
        both = held[i, :units].reshape(2 * units, width)
        result = lax.dot_general(
            both, rows_ref[...], (((1,), (1,)), ((), ())), preferred_element_type=F32
        )
        for part in range(mixed.shape[1]):
            turns = mixed.at[i % 2, part]
            turns[...] = result[:, part * 128 : part * 128 + 128]
            gate = turns[pl.ds(0, units, stride=2), :]
            up = turns[pl.ds(1, units, stride=2), :]
            act = (gate / (1.0 + jnp.exp(-gate)) * up).astype(BF16)
            acts[i, part * 128 : part * 128 + 128, :] = act.T
    tile = 256

    def one_tile(j, _):
        columns = pl.ds(pl.multiple_of(j * tile, tile), tile)
        total = None
        for i in range(count):
            down = held[i, units:, :, columns].reshape(units, tile)
            part = jnp.dot(acts[i], down, preferred_element_type=F32)
            total = part if total is None else total + part
        out_ref[:, columns] = total.astype(BF16)
        return 0

    lax.fori_loop(0, width // tile, one_tile, 0)


def run_experts(rows, sets, units):
    count = len(sets)
    width = rows.shape[1]
    vmem = pl.BlockSpec(memory_space=pltpu.VMEM)
    anywhere = pl.BlockSpec(memory_space=pl.ANY)
    pieces = [piece for pieces in sets for piece in pieces]
    return pl.pallas_call(
        functools.partial(experts_kernel, units, tuple(len(pieces) for pieces in sets)),
        out_shape=jax.ShapeDtypeStruct(rows.shape, BF16),
        in_specs=[vmem] + [anywhere] * len(pieces),
        out_specs=vmem,
        scratch_shapes=[
            pltpu.VMEM((count, units + units // 2, 2, width), BF16),
            pltpu.VMEM((2, rows.shape[0] // 128, 2 * units, 128), F32),
            pltpu.VMEM((count, rows.shape[0], units), BF16),
            pltpu.SemaphoreType.DMA((len(pieces),)),
        ],
        compiler_params=pltpu.CompilerParams(vmem_limit_bytes=52 << 20),
        cost_estimate=pl.CostEstimate(
            flops=6 * rows.shape[0] * width * units * count,
            bytes_accessed=6 * width * units * count,
            transcendentals=rows.shape[0] * units * count,
        ),
        name="experts",
    )(rows, *pieces)


def shards(
    tokens,
    norm_gain,
    w_qkv,
    w_out,
    moe_gain,
    w_router,
    gate_up,
    w_down,
    lengths,
    blocks_seen,
    expert_ids,
    old_place,
    new_place,
):
    block_rows = tokens.shape[0]
    model_width = tokens.shape[1]
    exp_count = lax.axis_size(EXP)
    block_index = lax.axis_index(SEQ)
    slot_index = lax.axis_index(EXP)
    heads_here = w_qkv.shape[2] // HEAD_DIM
    slice_width = gate_up.shape[3]
    shard_rows = block_rows // exp_count
    n_zh, n_x, n_c = lax.axis_size("zh"), lax.axis_size("x"), lax.axis_size("c")
    my_zh, my_x, my_c = lax.axis_index("zh"), lax.axis_index("x"), lax.axis_index("c")
    expert_count = w_router.shape[1]
    expert_range = jnp.arange(expert_count, dtype=I32)

    where = jnp.stack([my_zh, my_x, my_c]).astype(I32)

    by_unit = jnp.transpose(gate_up[0], (2, 0, 1))
    down = w_down[0]
    all_rows = jnp.concatenate([by_unit, down.reshape(slice_width // 2, 2, model_width)], axis=0)
    half = all_rows.shape[0] // 2
    first_rows, second_rows = all_rows[:half], all_rows[half:]
    first_left, first_right = shift(first_rows, "x", 1), shift(first_rows, "x", -1)

    slot_old = owner_table(old_place)
    source_slot = jnp.sum(
        jnp.where(new_place[:, None] == expert_range[None, :], slot_old[None, :], 0),
        axis=1,
        dtype=I32,
    )

    def spread_pieces(array, piece):
        spare = exp_count * piece - array.shape[0]
        padded = jnp.pad(array, ((0, spare),) + ((0, 0),) * (array.ndim - 1))
        split = padded.reshape((exp_count, piece) + array.shape[1:])
        return lax.all_to_all(split, EXP, 0, 0, tiled=True)

    def settle(ordered):
        moved = lax.all_to_all(ordered, EXP, 0, 0, tiled=True)
        return moved.reshape((-1,) + ordered.shape[2:])

    down_spread = spread_pieces(down, -(-slice_width // (8 * exp_count)) * 8)

    row_range = jnp.arange(block_rows, dtype=I32)
    my_places = row_places(lengths, block_index * block_rows + row_range)
    spacing = jnp.arange(HEAD_DIM // 2, dtype=F32) / (HEAD_DIM // 2)
    freqs_all = jnp.exp(-jnp.log(10000.0) * spacing)
    angles = my_places.astype(F32)[:, None] * freqs_all[None, :]
    cosine, sine = jnp.cos(angles), jnp.sin(angles)
    unseen = jnp.where(blocks_seen > 0, 0.0, masked_score)
    unseen = jnp.broadcast_to(unseen, (block_rows, unseen.shape[1]))
    ids_lanes = jnp.pad(
        expert_ids.astype(F32),
        ((0, block_rows - shard_rows), (0, HEAD_DIM - unseen.shape[1] - 2)),
    )
    extra = jnp.concatenate([jnp.zeros((block_rows, HEAD_DIM), F32), unseen, ids_lanes], axis=1)
    packed = project(
        where,
        tokens,
        norm_gain,
        jnp.transpose(w_qkv, (1, 0, 2)),
        jnp.concatenate([cosine] * 4, axis=1),
        jnp.concatenate([-sine, sine] * 2, axis=1),
        extra,
    )

    packets = [packed[0]] + [shift(packed[step], "zh", step) for step in range(1, n_zh)]
    pairs, queries, ids_rows = join_packets(packets, shard_rows)
    pairs, first_left, first_right, unit_rows, down_spread = tie(
        pairs, first_left, first_right, by_unit, down_spread
    )
    gate_spread = spread_pieces(unit_rows, -(-slice_width // exp_count))
    near = jnp.concatenate(gather_near(pairs, "x"), axis=0)
    near, second_rows = tie(near, second_rows)
    second_left, second_right = shift(second_rows, "x", 1), shift(second_rows, "x", -1)
    other = shift(near, "c", 1)
    attended = attend(where, lengths, queries, near, other, n_zh, n_x, n_c)
    attended, gate_spread = tie(attended, gate_spread)
    returned = [attended[0]] + [shift(attended[step], "zh", -step) for step in range(1, n_zh)]
    partial = output_projection(where, w_out, returned)
    partial = partial.reshape(exp_count, shard_rows, model_width)
    partial, first_left, second_left, second_right = tie(
        partial, first_left, second_left, second_right
    )
    first_far, second_far = shift(first_left, "x", 1), shift(second_right, "x", -1)

    partial = lax.all_to_all(partial, EXP, 0, 0, tiled=True)
    head_total = jnp.sum(partial.astype(F32), axis=0)
    residual = lax.dynamic_slice_in_dim(tokens, slot_index * shard_rows, shard_rows, 0)
    hidden = (residual.astype(F32) + head_total).astype(BF16)
    moe_in = rms_scale(hidden, moe_gain).astype(BF16)

    rows_near = jnp.concatenate(gather_near(moe_in, "zh"), axis=0)
    ids_near = ids_rows[:, 96:98].astype(F32).astype(I32)
    capacity = min(shard_rows, 4 * shard_rows // exp_count)
    near_rows = n_zh * shard_rows
    pair_ids = ids_near.reshape(n_zh, 2 * shard_rows)
    pair_marks = (pair_ids[:, :, None] == expert_range[None, None, :]).astype(I32)
    earlier = jnp.cumsum(pair_marks, axis=1, dtype=I32) - pair_marks
    rank_in = jnp.sum(earlier * pair_marks, axis=2, dtype=I32)
    owner_of = jnp.sum(pair_marks * slot_old[None, None, :], axis=2, dtype=I32)
    target = (owner_of * n_zh + jnp.arange(n_zh, dtype=I32)[:, None]) * capacity + rank_in
    target = target.reshape(near_rows, 2)
    slot_range = jnp.arange(exp_count * n_zh * capacity, dtype=I32)
    marks = target[:, :, None] == slot_range[None, None, :]
    selector = jnp.any(marks, axis=1).astype(BF16)
    outgoing = lax.dot_general(
        selector, rows_near, (((0,), (0,)), ((), ())), preferred_element_type=F32
    ).astype(BF16)
    gate_ordered, down_ordered = reorder(source_slot, gate_spread), reorder(source_slot, down_spread)
    outgoing, gate_ordered, down_ordered, first_far, second_far = tie(
        outgoing, gate_ordered, down_ordered, first_far, second_far
    )
    sets = [
        (first_rows, second_rows),
        (first_left, second_left),
        (first_right, second_right),
        (first_far, second_far),
    ]
    sets_other = [tuple(shift(piece, "c", 1) for piece in pieces) for pieces in sets]
    arrived = lax.all_to_all(
        outgoing.reshape(exp_count, n_zh * capacity, model_width), EXP, 0, 0, tiled=True
    ).reshape(-1, model_width)

    logits = jnp.dot(rows_near, w_router, preferred_element_type=F32)
    chosen = jnp.sum(
        jnp.where(ids_near[:, :, None] == expert_range[None, None, :], logits[:, None, :], 0.0),
        axis=2,
    )
    gate_first = 1.0 / (1.0 + jnp.exp(chosen[:, 1] - chosen[:, 0]))
    gate_second = 1.0 / (1.0 + jnp.exp(chosen[:, 0] - chosen[:, 1]))
    gating = jnp.stack([gate_first, gate_second], axis=1)
    spread = jnp.sum(jnp.where(marks, gating[:, :, None], 0.0), axis=1)

    arrived, gate_ordered = tie(arrived, gate_ordered)
    new_gate = settle(gate_ordered)
    parts = run_experts(arrived, sets + sets_other, slice_width)
    parts, new_gate = tie(parts, new_gate)
    back = lax.all_to_all(
        parts.reshape(exp_count, n_zh * capacity, model_width), EXP, 0, 0, tiled=True
    ).reshape(-1, model_width)
    back, down_ordered = tie(back, down_ordered)
    new_down = settle(down_ordered)
    combined = jnp.dot(spread, back.astype(F32), precision=lax.Precision.HIGHEST)
    combined = combined.astype(BF16).reshape(n_zh, shard_rows, model_width)
    moe_sum = combined[0].astype(F32)
    for step in range(1, n_zh):
        moe_sum = moe_sum + shift(combined[step], "zh", -step).astype(F32)
    layer_out = (hidden.astype(F32) + moe_sum).astype(BF16)

    new_gate_up = jnp.transpose(new_gate[:slice_width], (1, 2, 0))[None]
    new_down = new_down[:slice_width][None]
    return (layer_out, new_gate_up, new_down)


def solution(mesh):
    fine = Mesh(mesh.devices.reshape(4, 4, 2, 2, 4), SEQ + EXP)
    in_specs = (
        P(SEQ, None),
        P(),
        P(None, None, EXP),
        P(EXP, None),
        P(),
        P(),
        P(EXP, None, None, SEQ),
        P(EXP, SEQ, None),
        P(),
        P(SEQ, None),
        P(SEQ + EXP, None),
        P(),
        P(),
    )
    out_specs = (P(SEQ + EXP, None), P(EXP, None, None, SEQ), P(EXP, SEQ, None))
    return jax.shard_map(shards, mesh=fine, in_specs=in_specs, out_specs=out_specs, check_vma=False)
```

```python
import functools

import jax
import jax.numpy as jnp
from jax import lax
from jax.experimental import pallas as pl
from jax.experimental.pallas import tpu as pltpu
from jax.sharding import Mesh, PartitionSpec as P

HEAD_DIM = 64
SEQ = ("zh", "x", "c")
EXP = ("zl", "y")

epsilon = 1e-05
masked_score = -1e30
F32 = jnp.float32
BF16 = jnp.bfloat16
I32 = jnp.int32


def rms_scale(values_in, gain):
    widened = values_in.astype(F32)
    inverse = lax.rsqrt(jnp.mean(widened * widened, axis=-1, keepdims=True) + epsilon)
    return widened * inverse * gain.astype(F32)


def owner_table(placing):
    slot_range = jnp.arange(placing.shape[0], dtype=I32)
    return jnp.sum(
        jnp.where(placing[:, None] == slot_range[None, :], slot_range[:, None], 0),
        axis=0,
        dtype=I32,
    )


def shift(value, axis, by):
    count = lax.axis_size(axis)
    return lax.ppermute(value, axis, [(i, (i + by) % count) for i in range(count)])


def gather_near(value, axis):
    return [value] + [shift(value, axis, step) for step in range(1, lax.axis_size(axis))]


def tie(*values):
    return lax.optimization_barrier(values)


def attend_kernel(n_x, n_c, where_ref, lengths_ref, queries_ref, near_ref, other_ref, out_ref, held):
    n_zh, rows, _ = out_ref.shape
    my_zh, my_x, my_c = where_ref[0], where_ref[1], where_ref[2]
    lane = lax.broadcasted_iota(I32, (rows, 128), 1)
    column = lax.broadcasted_iota(I32, (1, rows), 1)
    row_iota = lax.broadcasted_iota(I32, (rows, 1), 0)

    def pair_of(dz, dc, dx):
        source = near_ref if dc == 0 else other_ref
        first = pl.multiple_of(dx * (n_zh * rows) + dz * rows, rows)
        return source[pl.ds(first, rows), :]

    for dq in range(n_zh):
        zh_q = lax.rem(my_zh - dq + n_zh, n_zh)
        row_ids = (zh_q * (n_x * n_c) + my_x * n_c + my_c) * rows + row_iota
        starts = jnp.zeros((rows, 1), I32)
        ending = 0
        for doc in range(lengths_ref.shape[0]):
            ending = ending + lengths_ref[doc]
            starts = jnp.where(row_ids >= ending, ending, starts)
        queries = queries_ref[dq * rows : (dq + 1) * rows, :]

        def score(dz, largest):
            zh_k = lax.rem(my_zh - dz + n_zh, n_zh)

            def run(largest):
                for dc in range(n_c):
                    at_c = lax.rem(my_c - dc + n_c, n_c)
                    for dx in range(n_x):
                        at_x = lax.rem(my_x - dx + n_x, n_x)
                        block = zh_k * (n_x * n_c) + at_x * n_c + at_c
                        mark = jnp.where(lane == block + HEAD_DIM, 1.0, 0.0).astype(BF16)
                        keys = jnp.where(lane < HEAD_DIM, pair_of(dz, dc, dx), mark)
                        scores = lax.dot_general(
                            queries, keys, (((1,), (1,)), ((), ())), preferred_element_type=F32
                        )
                        key_ids = block * rows + column
                        allowed = (key_ids >= starts) & (key_ids <= row_ids)
                        scores = jnp.where(allowed, scores, masked_score)
                        held[dz, dc * n_x + dx] = scores
                        largest = jnp.maximum(largest, scores)
                return largest

            return lax.cond(zh_k <= zh_q, run, lambda v: v, largest)

        largest = lax.fori_loop(
            0, n_zh, score, jnp.full((rows, 128), masked_score, F32)
        )
        top = jnp.max(largest, axis=1, keepdims=True)

        def mix(dz, state):
            zh_k = lax.rem(my_zh - dz + n_zh, n_zh)

            def run(state):
                totals, summed = state
                for dc in range(n_c):
                    for dx in range(n_x):
                        weights = jnp.exp(held[dz, dc * n_x + dx] - top)
                        totals = totals + weights
                        summed = summed + jnp.dot(
                            weights.astype(BF16), pair_of(dz, dc, dx), preferred_element_type=F32
                        )
                return totals, summed

            return lax.cond(zh_k <= zh_q, run, lambda v: v, state)

        nothing = jnp.zeros((rows, 128), F32)
        totals, summed = lax.fori_loop(0, n_zh, mix, (nothing, nothing))
        mixed = summed / jnp.sum(totals, axis=1, keepdims=True)
        out_ref[dq] = mixed[:, HEAD_DIM:].astype(BF16)


def attend(where, lengths, queries, near, other, n_zh, n_x, n_c):
    rows = queries.shape[0] // n_zh
    vmem = pl.BlockSpec(memory_space=pltpu.VMEM)
    smem = pl.BlockSpec(memory_space=pltpu.SMEM)
    keys = near.shape[0] * 2
    return pl.pallas_call(
        functools.partial(attend_kernel, n_x, n_c),
        out_shape=jax.ShapeDtypeStruct((n_zh, rows, HEAD_DIM), BF16),
        in_specs=[smem, smem, vmem, vmem, vmem],
        out_specs=vmem,
        scratch_shapes=[pltpu.VMEM((n_zh, n_c * n_x, rows, 128), F32)],
        compiler_params=pltpu.CompilerParams(vmem_limit_bytes=24 << 20),
        cost_estimate=pl.CostEstimate(
            flops=4 * n_zh * rows * keys * 128, bytes_accessed=2 << 20, transcendentals=n_zh * rows * keys
        ),
        name="attend",
    )(where, lengths, queries, near, other)


def project_kernel(where_ref, tokens_ref, gain_ref, weight_ref, cos_ref, sin_ref, extra_ref, *refs):
    outs, held = refs[:-1], refs[-1]
    widened = tokens_ref[...].astype(F32)
    inverse = lax.rsqrt(jnp.mean(widened * widened, axis=-1, keepdims=True) + epsilon)
    normed = (widened * inverse * gain_ref[...].astype(F32)).astype(BF16)
    q, k, v = (
        jnp.dot(normed, weight_ref[i], preferred_element_type=F32) for i in range(3)
    )
    rows, width = q.shape
    cosine = jnp.concatenate([cos_ref[...]] * (width // 128), axis=1)
    sine = jnp.concatenate([sin_ref[...]] * (width // 128), axis=1)
    lane = lax.broadcasted_iota(I32, (rows, width), 1)
    first_half = lax.rem(lane, HEAD_DIM) < HEAD_DIM // 2
    low = lax.broadcasted_iota(I32, (rows, 128), 1) < HEAD_DIM

    def rotated(value):
        ahead = pltpu.roll(value, width - HEAD_DIM // 2, 1)
        behind = pltpu.roll(value, HEAD_DIM // 2, 1)
        return value * cosine + jnp.where(first_half, ahead, behind) * sine

    q, k = rotated(q) * HEAD_DIM ** (-0.5), rotated(k)
    heads = len(outs)
    for head in range(heads):
        columns = slice(head // 2 * 128, head // 2 * 128 + 128)
        q_here, k_here, v_here = q[:, columns], k[:, columns], v[:, columns]
        if head % 2:
            q_here, k_here = pltpu.roll(q_here, HEAD_DIM, 1), pltpu.roll(k_here, HEAD_DIM, 1)
        else:
            v_here = pltpu.roll(v_here, HEAD_DIM, 1)
        held[head, :, :128] = jnp.where(low, q_here, extra_ref[...]).astype(BF16)
        held[head, :, 128:] = jnp.where(low, k_here, v_here).astype(BF16)
    for step in range(heads):
        outs[step][...] = held[lax.rem(where_ref[0] + step, heads)]


def project(where, tokens, gain, weight, cosine, sine, extra):
    rows, width = tokens.shape
    heads = weight.shape[2] // HEAD_DIM
    vmem = pl.BlockSpec(memory_space=pltpu.VMEM)
    packet = jax.ShapeDtypeStruct((rows, 256), BF16)
    return pl.pallas_call(
        project_kernel,
        out_shape=[packet] * heads,
        in_specs=[pl.BlockSpec(memory_space=pltpu.SMEM)] + [vmem] * 6,
        out_specs=[vmem] * heads,
        scratch_shapes=[pltpu.VMEM((heads, rows, 256), BF16)],
        compiler_params=pltpu.CompilerParams(vmem_limit_bytes=24 << 20),
        cost_estimate=pl.CostEstimate(
            flops=6 * rows * width * heads * HEAD_DIM,
            bytes_accessed=2 * weight.size + 2 * tokens.size,
            transcendentals=0,
        ),
        name="project",
    )(where, tokens, gain[None], weight, cosine, sine, extra)


def join_kernel(*refs):
    pairs_ref, queries_ref, ids_ref = refs[-3:]
    count = len(refs) - 3
    rows, few = refs[0].shape[0], ids_ref.shape[0] // count
    for i, ref in enumerate(refs[:-3]):
        pairs_ref[i * rows : (i + 1) * rows, :] = ref[:, 128:]
        queries_ref[i * rows : (i + 1) * rows, :] = ref[:, :128]
        ids_ref[i * few : (i + 1) * few, :] = ref[:few, :128]


def join_packets(packets, few):
    rows, count = packets[0].shape[0], len(packets)
    vmem = pl.BlockSpec(memory_space=pltpu.VMEM)
    return pl.pallas_call(
        join_kernel,
        out_shape=[
            jax.ShapeDtypeStruct((count * rows, 128), BF16),
            jax.ShapeDtypeStruct((count * rows, 128), BF16),
            jax.ShapeDtypeStruct((count * few, 128), BF16),
        ],
        in_specs=[vmem] * count,
        out_specs=[vmem] * 3,
        name="join",
    )(*packets)


def output_kernel(where_ref, weight_ref, *refs):
    out_ref = refs[-1]
    heads = len(refs) - 1
    total = None
    for step in range(heads):
        head = lax.rem(where_ref[0] + step, heads)
        weight = weight_ref[pl.ds(pl.multiple_of(head * HEAD_DIM, HEAD_DIM), HEAD_DIM), :]
        part = jnp.dot(refs[step][...], weight, preferred_element_type=F32)
        total = part if total is None else total + part
    out_ref[...] = total.astype(BF16)


def output_projection(where, weight, returned):
    rows = returned[0].shape[0]
    vmem = pl.BlockSpec(memory_space=pltpu.VMEM)
    return pl.pallas_call(
        output_kernel,
        out_shape=jax.ShapeDtypeStruct((rows, weight.shape[1]), BF16),
        in_specs=[pl.BlockSpec(memory_space=pltpu.SMEM)] + [vmem] * (1 + len(returned)),
        out_specs=vmem,
        compiler_params=pltpu.CompilerParams(vmem_limit_bytes=16 << 20),
        cost_estimate=pl.CostEstimate(
            flops=2 * rows * weight.size, bytes_accessed=2 * weight.size, transcendentals=0
        ),
        name="output",
    )(where, weight, *returned)


def reorder_kernel(order_ref, gate_ref, down_ref, out_ref, held, sems):
    count, gate_rows = gate_ref.shape[:2]
    down_rows, width = held.shape[1:]
    copies = []
    for i in range(count):
        source = order_ref[i]
        copies.append(pltpu.make_async_copy(down_ref.at[source], held.at[i], sems.at[0, i]))
        copies.append(
            pltpu.make_async_copy(
                gate_ref.at[source], out_ref.at[i, pl.ds(0, gate_rows)], sems.at[1, i]
            )
        )
    for copy in copies:
        copy.start()
    for i in range(count):
        copies[2 * i].wait()
        out_ref[i, gate_rows:] = held[i].reshape(down_rows // 2, 2, width)
    for i in range(count):
        copies[2 * i + 1].wait()


def reorder(order, gate, down):
    count, gate_rows, _, width = gate.shape
    down_rows = down.shape[1]
    anywhere = pl.BlockSpec(memory_space=pl.ANY)
    return pl.pallas_call(
        reorder_kernel,
        out_shape=jax.ShapeDtypeStruct((count, gate_rows + down_rows // 2, 2, width), BF16),
        in_specs=[pl.BlockSpec(memory_space=pltpu.SMEM), anywhere, anywhere],
        out_specs=pl.BlockSpec(memory_space=pltpu.VMEM),
        scratch_shapes=[
            pltpu.VMEM((count, down_rows, width), BF16),
            pltpu.SemaphoreType.DMA((2, count)),
        ],
        cost_estimate=pl.CostEstimate(
            flops=0, bytes_accessed=4 * (gate.size + down.size), transcendentals=0
        ),
        name="reorder",
    )(order, gate, down)


def second_kernel(first, by_unit_ref, down_ref, out_ref, sem):
    units = by_unit_ref.shape[0] - first
    copy = pltpu.make_async_copy(by_unit_ref.at[pl.ds(first, units)], out_ref.at[pl.ds(0, units)], sem)
    copy.start()
    out_ref[units:] = down_ref[...].reshape(down_ref.shape[0] // 2, 2, down_ref.shape[1])
    copy.wait()


def second_half(by_unit, down, first):
    units, _, width = by_unit.shape
    return pl.pallas_call(
        functools.partial(second_kernel, first),
        out_shape=jax.ShapeDtypeStruct((units - first + units // 2, 2, width), BF16),
        in_specs=[pl.BlockSpec(memory_space=pl.ANY), pl.BlockSpec(memory_space=pltpu.VMEM)],
        out_specs=pl.BlockSpec(memory_space=pltpu.VMEM),
        scratch_shapes=[pltpu.SemaphoreType.DMA],
        cost_estimate=pl.CostEstimate(flops=0, bytes_accessed=6 * down.size, transcendentals=0),
        name="second",
    )(by_unit, down)


def experts_kernel(units, parts, *refs):
    rows_ref = refs[0]
    pieces, count = refs[1 : 1 + sum(parts)], len(parts)
    out_ref, held, mixed, acts, sems = refs[1 + len(pieces) :]
    width = held.shape[3]
    copies, used = [], 0
    for i in range(count):
        first = 0
        for ref in pieces[used : used + parts[i]]:
            last = first + ref.shape[0]
            copies.append(pltpu.make_async_copy(ref, held.at[i, first:last], sems.at[len(copies)]))
            first = last
        used += parts[i]
    for copy in copies:
        copy.start()
    used = 0
    for i in range(count + 1):
        if i < count:
            for copy in copies[used : used + parts[i]]:
                copy.wait()
            used += parts[i]
            both = held[i, :units].reshape(2 * units, width)
            result = lax.dot_general(
                both, rows_ref[...], (((1,), (1,)), ((), ())), preferred_element_type=F32
            )
        if i > 0:
            for part in range(mixed.shape[1]):
                turns = mixed.at[(i - 1) % 2, part]
                gate = turns[pl.ds(0, units, stride=2), :]
                up = turns[pl.ds(1, units, stride=2), :]
                act = (gate / (1.0 + jnp.exp(-gate)) * up).astype(BF16)
                acts[i - 1, part * 128 : part * 128 + 128, :] = act.T
        if i < count:
            for part in range(mixed.shape[1]):
                mixed[i % 2, part] = result[:, part * 128 : part * 128 + 128]
    tile = 256

    def one_tile(j, _):
        columns = pl.ds(pl.multiple_of(j * tile, tile), tile)
        total = None
        for i in range(count):
            down = held[i, units:, :, columns].reshape(units, tile)
            part = jnp.dot(acts[i], down, preferred_element_type=F32)
            total = part if total is None else total + part
        out_ref[:, columns] = total.astype(BF16)
        return 0

    lax.fori_loop(0, width // tile, one_tile, 0)


def run_experts(rows, sets, units):
    count = len(sets)
    width = rows.shape[1]
    vmem = pl.BlockSpec(memory_space=pltpu.VMEM)
    anywhere = pl.BlockSpec(memory_space=pl.ANY)
    pieces = [piece for pieces in sets for piece in pieces]
    return pl.pallas_call(
        functools.partial(experts_kernel, units, tuple(len(pieces) for pieces in sets)),
        out_shape=jax.ShapeDtypeStruct(rows.shape, BF16),
        in_specs=[vmem] + [anywhere] * len(pieces),
        out_specs=vmem,
        scratch_shapes=[
            pltpu.VMEM((count, units + units // 2, 2, width), BF16),
            pltpu.VMEM((2, rows.shape[0] // 128, 2 * units, 128), F32),
            pltpu.VMEM((count, rows.shape[0], units), BF16),
            pltpu.SemaphoreType.DMA((len(pieces),)),
        ],
        compiler_params=pltpu.CompilerParams(vmem_limit_bytes=52 << 20),
        cost_estimate=pl.CostEstimate(
            flops=6 * rows.shape[0] * width * units * count,
            bytes_accessed=6 * width * units * count,
            transcendentals=rows.shape[0] * units * count,
        ),
        name="experts",
    )(rows, *pieces)


def shards(
    tokens,
    norm_gain,
    w_qkv,
    w_out,
    moe_gain,
    w_router,
    gate_up,
    w_down,
    lengths,
    blocks_seen,
    expert_ids,
    old_place,
    new_place,
):
    block_rows = tokens.shape[0]
    model_width = tokens.shape[1]
    exp_count = lax.axis_size(EXP)
    block_index = lax.axis_index(SEQ)
    slot_index = lax.axis_index(EXP)
    heads_here = w_qkv.shape[2] // HEAD_DIM
    slice_width = gate_up.shape[3]
    shard_rows = block_rows // exp_count
    n_zh, n_x, n_c = lax.axis_size("zh"), lax.axis_size("x"), lax.axis_size("c")
    my_zh, my_x, my_c = lax.axis_index("zh"), lax.axis_index("x"), lax.axis_index("c")
    expert_count = w_router.shape[1]
    expert_range = jnp.arange(expert_count, dtype=I32)

    where = jnp.stack([my_zh, my_x, my_c]).astype(I32)

    by_unit = jnp.transpose(gate_up[0], (2, 0, 1))
    down = w_down[0]
    half = (slice_width + slice_width // 2) // 2
    first_rows = by_unit[:half]
    second_rows = second_half(by_unit, down, half)
    first_left, first_right = shift(first_rows, "x", 1), shift(first_rows, "x", -1)

    slot_old = owner_table(old_place)
    source_slot = jnp.sum(
        jnp.where(new_place[:, None] == expert_range[None, :], slot_old[None, :], 0),
        axis=1,
        dtype=I32,
    )

    def spread_pieces(array, piece):
        spare = exp_count * piece - array.shape[0]
        padded = jnp.pad(array, ((0, spare),) + ((0, 0),) * (array.ndim - 1))
        split = padded.reshape((exp_count, piece) + array.shape[1:])
        return lax.all_to_all(split, EXP, 0, 0, tiled=True)

    down_spread = spread_pieces(down, -(-slice_width // (8 * exp_count)) * 8)

    row_ids = block_index * block_rows + jnp.arange(block_rows, dtype=I32)[:, None]
    docs = jnp.arange(lengths.shape[0], dtype=I32)
    ending = jnp.sum(jnp.where(docs[None, :] <= docs[:, None], lengths[None, :], 0), axis=1)
    starts = jnp.max(jnp.where(row_ids >= ending[None, :], ending[None, :], 0), axis=1)[:, None]
    lanes = jnp.arange(128, dtype=I32)[None, :]
    spacing = (lanes % (HEAD_DIM // 2)).astype(F32) / (HEAD_DIM // 2)
    angles = (row_ids - starts).astype(F32) * jnp.exp(-jnp.log(10000.0) * spacing)
    cosine = jnp.cos(angles)
    sine = jnp.where(lanes % HEAD_DIM < HEAD_DIM // 2, -1.0, 1.0) * jnp.sin(angles)
    unseen = jnp.where(blocks_seen > 0, 0.0, masked_score)
    unseen = jnp.broadcast_to(unseen, (block_rows, unseen.shape[1]))
    ids_lanes = jnp.pad(
        expert_ids.astype(F32),
        ((0, block_rows - shard_rows), (0, HEAD_DIM - unseen.shape[1] - 2)),
    )
    extra = jnp.concatenate([jnp.zeros((block_rows, HEAD_DIM), F32), unseen, ids_lanes], axis=1)
    packed = project(
        where,
        tokens,
        norm_gain,
        jnp.transpose(w_qkv, (1, 0, 2)),
        cosine,
        sine,
        extra,
    )

    packets = [packed[0]] + [shift(packed[step], "zh", step) for step in range(1, n_zh)]
    pairs, queries, ids_rows = join_packets(packets, shard_rows)
    pairs, first_left, first_right, unit_rows, down_spread = tie(
        pairs, first_left, first_right, by_unit, down_spread
    )
    gate_piece = -(-slice_width // exp_count)
    gate_spread = spread_pieces(unit_rows, gate_piece)
    near = jnp.concatenate(gather_near(pairs, "x"), axis=0)
    near, second_rows = tie(near, second_rows)
    second_left, second_right = shift(second_rows, "x", 1), shift(second_rows, "x", -1)
    other = shift(near, "c", 1)
    attended = attend(where, lengths, queries, near, other, n_zh, n_x, n_c)
    attended, gate_spread = tie(attended, gate_spread)
    returned = [attended[0]] + [shift(attended[step], "zh", -step) for step in range(1, n_zh)]
    partial = output_projection(where, w_out, returned)
    partial = partial.reshape(exp_count, shard_rows, model_width)
    partial, first_left, second_left, second_right = tie(
        partial, first_left, second_left, second_right
    )
    first_far, second_far = shift(first_left, "x", 1), shift(second_right, "x", -1)

    partial = lax.all_to_all(partial, EXP, 0, 0, tiled=True)
    first_other, second_other = shift(first_rows, "c", 1), shift(second_rows, "c", 1)
    partial, first_other, second_other = tie(partial, first_other, second_other)
    head_total = jnp.sum(partial.astype(F32), axis=0)
    residual = lax.dynamic_slice_in_dim(tokens, slot_index * shard_rows, shard_rows, 0)
    hidden = (residual.astype(F32) + head_total).astype(BF16)
    moe_in = rms_scale(hidden, moe_gain).astype(BF16)

    rows_near = jnp.concatenate(gather_near(moe_in, "zh"), axis=0)
    ids_near = ids_rows[:, 96:98].astype(F32).astype(I32)
    capacity = min(shard_rows, 4 * shard_rows // exp_count)
    near_rows = n_zh * shard_rows
    pair_ids = ids_near.reshape(n_zh, 2 * shard_rows)
    pair_marks = (pair_ids[:, :, None] == expert_range[None, None, :]).astype(I32)
    earlier = jnp.cumsum(pair_marks, axis=1, dtype=I32) - pair_marks
    rank_in = jnp.sum(earlier * pair_marks, axis=2, dtype=I32)
    owner_of = jnp.sum(pair_marks * slot_old[None, None, :], axis=2, dtype=I32)
    target = (owner_of * n_zh + jnp.arange(n_zh, dtype=I32)[:, None]) * capacity + rank_in
    target = target.reshape(near_rows, 2)
    slot_range = jnp.arange(exp_count * n_zh * capacity, dtype=I32)
    marks = target[:, :, None] == slot_range[None, None, :]
    selector = jnp.any(marks, axis=1).astype(BF16)
    outgoing = lax.dot_general(
        selector, rows_near, (((0,), (0,)), ((), ())), preferred_element_type=F32
    ).astype(BF16)
    ordered = reorder(source_slot, gate_spread, down_spread)
    outgoing, ordered, first_far, second_far = tie(outgoing, ordered, first_far, second_far)
    sets = [
        (first_rows, second_rows),
        (first_left, second_left),
        (first_right, second_right),
        (first_far, second_far),
    ]
    sets_other = [(first_other, second_other)]
    sets_other += [tuple(shift(piece, "c", 1) for piece in pieces) for pieces in sets[1:]]
    arrived = lax.all_to_all(
        outgoing.reshape(exp_count, n_zh * capacity, model_width), EXP, 0, 0, tiled=True
    ).reshape(-1, model_width)

    logits = jnp.dot(rows_near, w_router, preferred_element_type=F32)
    chosen = jnp.sum(
        jnp.where(ids_near[:, :, None] == expert_range[None, None, :], logits[:, None, :], 0.0),
        axis=2,
    )
    gate_first = 1.0 / (1.0 + jnp.exp(chosen[:, 1] - chosen[:, 0]))
    gate_second = 1.0 / (1.0 + jnp.exp(chosen[:, 0] - chosen[:, 1]))
    gating = jnp.stack([gate_first, gate_second], axis=1)
    spread = jnp.sum(jnp.where(marks, gating[:, :, None], 0.0), axis=1)

    arrived, ordered = tie(arrived, ordered)
    moved = lax.all_to_all(ordered, EXP, 0, 0, tiled=True)
    parts = run_experts(arrived, sets + sets_other, slice_width)
    parts, moved = tie(parts, moved)
    back = lax.all_to_all(
        parts.reshape(exp_count, n_zh * capacity, model_width), EXP, 0, 0, tiled=True
    ).reshape(-1, model_width)
    combined = jnp.dot(spread, back.astype(F32), precision=lax.Precision.HIGHEST)
    combined = combined.astype(BF16)
    combined = combined.reshape(n_zh, shard_rows, model_width)
    moe_sum = combined[0].astype(F32)
    for step in range(1, n_zh):
        moe_sum = moe_sum + shift(combined[step], "zh", -step).astype(F32)
    layer_out = (hidden.astype(F32) + moe_sum).astype(BF16)

    new_gate = moved[:, :gate_piece].reshape(-1, 2, model_width)[:slice_width]
    new_down = moved[:, gate_piece:].reshape(-1, model_width)[:slice_width]
    new_gate_up, new_down = jnp.transpose(new_gate, (1, 2, 0))[None], new_down[None]
    return (layer_out, new_gate_up, new_down)


def solution(mesh):
    fine = Mesh(mesh.devices.reshape(4, 4, 2, 2, 4), SEQ + EXP)
    in_specs = (
        P(SEQ, None),
        P(),
        P(None, None, EXP),
        P(EXP, None),
        P(),
        P(),
        P(EXP, None, None, SEQ),
        P(EXP, SEQ, None),
        P(),
        P(SEQ, None),
        P(SEQ + EXP, None),
        P(),
        P(),
    )
    out_specs = (P(SEQ + EXP, None), P(EXP, None, None, SEQ), P(EXP, SEQ, None))
    return jax.shard_map(shards, mesh=fine, in_specs=in_specs, out_specs=out_specs, check_vma=False)
```

```python
import functools

import jax
import jax.numpy as jnp
from jax import lax
from jax.experimental import pallas as pl
from jax.experimental.pallas import tpu as pltpu
from jax.sharding import Mesh, PartitionSpec as P

HEAD_DIM = 64
SEQ = ("zh", "x", "c")
EXP = ("zl", "y")

epsilon = 1e-05
masked_score = -1e30
F32 = jnp.float32
BF16 = jnp.bfloat16
I32 = jnp.int32


def rms_scale(values_in, gain):
    widened = values_in.astype(F32)
    inverse = lax.rsqrt(jnp.mean(widened * widened, axis=-1, keepdims=True) + epsilon)
    return widened * inverse * gain.astype(F32)


def owner_table(placing):
    slot_range = jnp.arange(placing.shape[0], dtype=I32)
    return jnp.sum(
        jnp.where(placing[:, None] == slot_range[None, :], slot_range[:, None], 0),
        axis=0,
        dtype=I32,
    )


def shift(value, axis, by):
    count = lax.axis_size(axis)
    return lax.ppermute(value, axis, [(i, (i + by) % count) for i in range(count)])


def gather_near(value, axis):
    return [value] + [shift(value, axis, step) for step in range(1, lax.axis_size(axis))]


def tie(*values):
    return lax.optimization_barrier(values)


def attend_kernel(n_x, n_c, where_ref, lengths_ref, queries_ref, near_ref, other_ref, out_ref, held):
    n_zh, rows, _ = out_ref.shape
    my_zh, my_x, my_c = where_ref[0], where_ref[1], where_ref[2]
    lane = lax.broadcasted_iota(I32, (rows, 128), 1)
    column = lax.broadcasted_iota(I32, (1, rows), 1)
    row_iota = lax.broadcasted_iota(I32, (rows, 1), 0)

    def pair_of(dz, dc, dx):
        source = near_ref if dc == 0 else other_ref
        first = pl.multiple_of(dx * (n_zh * rows) + dz * rows, rows)
        return source[pl.ds(first, rows), :]

    for dq in range(n_zh):
        zh_q = lax.rem(my_zh - dq + n_zh, n_zh)
        row_ids = (zh_q * (n_x * n_c) + my_x * n_c + my_c) * rows + row_iota
        starts = jnp.zeros((rows, 1), I32)
        ending = 0
        for doc in range(lengths_ref.shape[0]):
            ending = ending + lengths_ref[doc]
            starts = jnp.where(row_ids >= ending, ending, starts)
        queries = queries_ref[dq * rows : (dq + 1) * rows, :]

        def score(dz, largest):
            zh_k = lax.rem(my_zh - dz + n_zh, n_zh)

            def run(largest):
                for dc in range(n_c):
                    at_c = lax.rem(my_c - dc + n_c, n_c)
                    for dx in range(n_x):
                        at_x = lax.rem(my_x - dx + n_x, n_x)
                        block = zh_k * (n_x * n_c) + at_x * n_c + at_c
                        mark = jnp.where(lane == block + HEAD_DIM, 1.0, 0.0).astype(BF16)
                        keys = jnp.where(lane < HEAD_DIM, pair_of(dz, dc, dx), mark)
                        scores = lax.dot_general(
                            queries, keys, (((1,), (1,)), ((), ())), preferred_element_type=F32
                        )
                        key_ids = block * rows + column
                        allowed = (key_ids >= starts) & (key_ids <= row_ids)
                        scores = jnp.where(allowed, scores, masked_score)
                        held[dz, dc * n_x + dx] = scores
                        largest = jnp.maximum(largest, scores)
                return largest

            return lax.cond(zh_k <= zh_q, run, lambda v: v, largest)

        largest = lax.fori_loop(
            0, n_zh, score, jnp.full((rows, 128), masked_score, F32)
        )
        top = jnp.max(largest, axis=1, keepdims=True)

        def mix(dz, state):
            zh_k = lax.rem(my_zh - dz + n_zh, n_zh)

            def run(state):
                totals, summed = state
                for dc in range(n_c):
                    for dx in range(n_x):
                        weights = jnp.exp(held[dz, dc * n_x + dx] - top)
                        totals = totals + weights
                        summed = summed + jnp.dot(
                            weights.astype(BF16), pair_of(dz, dc, dx), preferred_element_type=F32
                        )
                return totals, summed

            return lax.cond(zh_k <= zh_q, run, lambda v: v, state)

        nothing = jnp.zeros((rows, 128), F32)
        totals, summed = lax.fori_loop(0, n_zh, mix, (nothing, nothing))
        mixed = summed / jnp.sum(totals, axis=1, keepdims=True)
        out_ref[dq] = mixed[:, HEAD_DIM:].astype(BF16)


def attend(where, lengths, queries, near, other, n_zh, n_x, n_c):
    rows = queries.shape[0] // n_zh
    vmem = pl.BlockSpec(memory_space=pltpu.VMEM)
    smem = pl.BlockSpec(memory_space=pltpu.SMEM)
    keys = near.shape[0] * 2
    return pl.pallas_call(
        functools.partial(attend_kernel, n_x, n_c),
        out_shape=jax.ShapeDtypeStruct((n_zh, rows, HEAD_DIM), BF16),
        in_specs=[smem, smem, vmem, vmem, vmem],
        out_specs=vmem,
        scratch_shapes=[pltpu.VMEM((n_zh, n_c * n_x, rows, 128), F32)],
        compiler_params=pltpu.CompilerParams(vmem_limit_bytes=24 << 20),
        cost_estimate=pl.CostEstimate(
            flops=4 * n_zh * rows * keys * 128, bytes_accessed=2 << 20, transcendentals=n_zh * rows * keys
        ),
        name="attend",
    )(where, lengths, queries, near, other)


def project_kernel(where_ref, tokens_ref, gain_ref, weight_ref, cos_ref, sin_ref, extra_ref, *refs):
    outs, held = refs[:-1], refs[-1]
    widened = tokens_ref[...].astype(F32)
    inverse = lax.rsqrt(jnp.mean(widened * widened, axis=-1, keepdims=True) + epsilon)
    normed = (widened * inverse * gain_ref[...].astype(F32)).astype(BF16)
    q, k, v = (
        jnp.dot(normed, weight_ref[i], preferred_element_type=F32) for i in range(3)
    )
    rows, width = q.shape
    cosine = jnp.concatenate([cos_ref[...]] * (width // 128), axis=1)
    sine = jnp.concatenate([sin_ref[...]] * (width // 128), axis=1)
    lane = lax.broadcasted_iota(I32, (rows, width), 1)
    first_half = lax.rem(lane, HEAD_DIM) < HEAD_DIM // 2
    low = lax.broadcasted_iota(I32, (rows, 128), 1) < HEAD_DIM

    def rotated(value):
        ahead = pltpu.roll(value, width - HEAD_DIM // 2, 1)
        behind = pltpu.roll(value, HEAD_DIM // 2, 1)
        return value * cosine + jnp.where(first_half, ahead, behind) * sine

    q, k = rotated(q) * HEAD_DIM ** (-0.5), rotated(k)
    heads = len(outs)
    for head in range(heads):
        columns = slice(head // 2 * 128, head // 2 * 128 + 128)
        q_here, k_here, v_here = q[:, columns], k[:, columns], v[:, columns]
        if head % 2:
            q_here, k_here = pltpu.roll(q_here, HEAD_DIM, 1), pltpu.roll(k_here, HEAD_DIM, 1)
        else:
            v_here = pltpu.roll(v_here, HEAD_DIM, 1)
        held[head, :, :128] = jnp.where(low, q_here, extra_ref[...]).astype(BF16)
        held[head, :, 128:] = jnp.where(low, k_here, v_here).astype(BF16)
    for step in range(heads):
        outs[step][...] = held[lax.rem(where_ref[0] + step, heads)]


def project(where, tokens, gain, weight, cosine, sine, extra):
    rows, width = tokens.shape
    heads = weight.shape[2] // HEAD_DIM
    vmem = pl.BlockSpec(memory_space=pltpu.VMEM)
    packet = jax.ShapeDtypeStruct((rows, 256), BF16)
    return pl.pallas_call(
        project_kernel,
        out_shape=[packet] * heads,
        in_specs=[pl.BlockSpec(memory_space=pltpu.SMEM)] + [vmem] * 6,
        out_specs=[vmem] * heads,
        scratch_shapes=[pltpu.VMEM((heads, rows, 256), BF16)],
        compiler_params=pltpu.CompilerParams(vmem_limit_bytes=24 << 20),
        cost_estimate=pl.CostEstimate(
            flops=6 * rows * width * heads * HEAD_DIM,
            bytes_accessed=2 * weight.size + 2 * tokens.size,
            transcendentals=0,
        ),
        name="project",
    )(where, tokens, gain[None], weight, cosine, sine, extra)


def join_kernel(*refs):
    pairs_ref, queries_ref, ids_ref = refs[-3:]
    count = len(refs) - 3
    rows, few = refs[0].shape[0], ids_ref.shape[0] // count
    for i, ref in enumerate(refs[:-3]):
        pairs_ref[i * rows : (i + 1) * rows, :] = ref[:, 128:]
        queries_ref[i * rows : (i + 1) * rows, :] = ref[:, :128]
        ids_ref[i * few : (i + 1) * few, :] = ref[:few, :128]


def join_packets(packets, few):
    rows, count = packets[0].shape[0], len(packets)
    vmem = pl.BlockSpec(memory_space=pltpu.VMEM)
    return pl.pallas_call(
        join_kernel,
        out_shape=[
            jax.ShapeDtypeStruct((count * rows, 128), BF16),
            jax.ShapeDtypeStruct((count * rows, 128), BF16),
            jax.ShapeDtypeStruct((count * few, 128), BF16),
        ],
        in_specs=[vmem] * count,
        out_specs=[vmem] * 3,
        name="join",
    )(*packets)


def output_kernel(where_ref, weight_ref, *refs):
    out_ref = refs[-1]
    heads = len(refs) - 1
    total = None
    for step in range(heads):
        head = lax.rem(where_ref[0] + step, heads)
        weight = weight_ref[pl.ds(pl.multiple_of(head * HEAD_DIM, HEAD_DIM), HEAD_DIM), :]
        part = jnp.dot(refs[step][...], weight, preferred_element_type=F32)
        total = part if total is None else total + part
    out_ref[...] = total.astype(BF16)


def output_projection(where, weight, returned):
    rows = returned[0].shape[0]
    vmem = pl.BlockSpec(memory_space=pltpu.VMEM)
    return pl.pallas_call(
        output_kernel,
        out_shape=jax.ShapeDtypeStruct((rows, weight.shape[1]), BF16),
        in_specs=[pl.BlockSpec(memory_space=pltpu.SMEM)] + [vmem] * (1 + len(returned)),
        out_specs=vmem,
        compiler_params=pltpu.CompilerParams(vmem_limit_bytes=16 << 20),
        cost_estimate=pl.CostEstimate(
            flops=2 * rows * weight.size, bytes_accessed=2 * weight.size, transcendentals=0
        ),
        name="output",
    )(where, weight, *returned)


def reorder_kernel(order_ref, gate_ref, down_ref, out_ref, held, sems):
    count, gate_rows = gate_ref.shape[:2]
    down_rows, width = held.shape[1:]
    copies = []
    for i in range(count):
        source = order_ref[i]
        copies.append(pltpu.make_async_copy(down_ref.at[source], held.at[i], sems.at[0, i]))
        copies.append(
            pltpu.make_async_copy(
                gate_ref.at[source], out_ref.at[i, pl.ds(0, gate_rows)], sems.at[1, i]
            )
        )
    for copy in copies:
        copy.start()
    for i in range(count):
        copies[2 * i].wait()
        out_ref[i, gate_rows:] = held[i].reshape(down_rows // 2, 2, width)
    for i in range(count):
        copies[2 * i + 1].wait()


def reorder(order, gate, down):
    count, gate_rows, _, width = gate.shape
    down_rows = down.shape[1]
    anywhere = pl.BlockSpec(memory_space=pl.ANY)
    return pl.pallas_call(
        reorder_kernel,
        out_shape=jax.ShapeDtypeStruct((count, gate_rows + down_rows // 2, 2, width), BF16),
        in_specs=[pl.BlockSpec(memory_space=pltpu.SMEM), anywhere, anywhere],
        out_specs=pl.BlockSpec(memory_space=pltpu.VMEM),
        scratch_shapes=[
            pltpu.VMEM((count, down_rows, width), BF16),
            pltpu.SemaphoreType.DMA((2, count)),
        ],
        cost_estimate=pl.CostEstimate(
            flops=0, bytes_accessed=4 * (gate.size + down.size), transcendentals=0
        ),
        name="reorder",
    )(order, gate, down)


def second_kernel(first, by_unit_ref, down_ref, out_ref, sem):
    units = by_unit_ref.shape[0] - first
    copy = pltpu.make_async_copy(by_unit_ref.at[pl.ds(first, units)], out_ref.at[pl.ds(0, units)], sem)
    copy.start()
    out_ref[units:] = down_ref[...].reshape(down_ref.shape[0] // 2, 2, down_ref.shape[1])
    copy.wait()


def second_half(by_unit, down, first):
    units, _, width = by_unit.shape
    return pl.pallas_call(
        functools.partial(second_kernel, first),
        out_shape=jax.ShapeDtypeStruct((units - first + units // 2, 2, width), BF16),
        in_specs=[pl.BlockSpec(memory_space=pl.ANY), pl.BlockSpec(memory_space=pltpu.VMEM)],
        out_specs=pl.BlockSpec(memory_space=pltpu.VMEM),
        scratch_shapes=[pltpu.SemaphoreType.DMA],
        cost_estimate=pl.CostEstimate(flops=0, bytes_accessed=6 * down.size, transcendentals=0),
        name="second",
    )(by_unit, down)


def experts_kernel(units, parts, *refs):
    rows_ref = refs[0]
    pieces, count = refs[1 : 1 + sum(parts)], len(parts)
    out_ref, held, mixed, acts, sems = refs[1 + len(pieces) :]
    width = held.shape[3]
    copies, used = [], 0
    for i in range(count):
        first = 0
        for ref in pieces[used : used + parts[i]]:
            last = first + ref.shape[0]
            copies.append(pltpu.make_async_copy(ref, held.at[i, first:last], sems.at[len(copies)]))
            first = last
        used += parts[i]
    for copy in copies:
        copy.start()
    used = 0
    for i in range(count + 1):
        if i < count:
            for copy in copies[used : used + parts[i]]:
                copy.wait()
            used += parts[i]
            both = held[i, :units].reshape(2 * units, width)
            result = lax.dot_general(
                both, rows_ref[...], (((1,), (1,)), ((), ())), preferred_element_type=F32
            )
        if i > 0:
            for part in range(mixed.shape[1]):
                turns = mixed.at[(i - 1) % 2, part]
                gate = turns[pl.ds(0, units, stride=2), :]
                up = turns[pl.ds(1, units, stride=2), :]
                act = (gate / (1.0 + jnp.exp(-gate)) * up).astype(BF16)
                acts[i - 1, part * 128 : part * 128 + 128, :] = act.T
        if i < count:
            for part in range(mixed.shape[1]):
                mixed[i % 2, part] = result[:, part * 128 : part * 128 + 128]
    tile = 256

    def one_tile(j, _):
        columns = pl.ds(pl.multiple_of(j * tile, tile), tile)
        total = None
        for i in range(count):
            down = held[i, units:, :, columns].reshape(units, tile)
            part = jnp.dot(acts[i], down, preferred_element_type=F32)
            total = part if total is None else total + part
        out_ref[:, columns] = total.astype(BF16)
        return 0

    lax.fori_loop(0, width // tile, one_tile, 0)


def run_experts(rows, sets, units):
    count = len(sets)
    width = rows.shape[1]
    vmem = pl.BlockSpec(memory_space=pltpu.VMEM)
    anywhere = pl.BlockSpec(memory_space=pl.ANY)
    pieces = [piece for pieces in sets for piece in pieces]
    return pl.pallas_call(
        functools.partial(experts_kernel, units, tuple(len(pieces) for pieces in sets)),
        out_shape=jax.ShapeDtypeStruct(rows.shape, BF16),
        in_specs=[vmem] + [anywhere] * len(pieces),
        out_specs=vmem,
        scratch_shapes=[
            pltpu.VMEM((count, units + units // 2, 2, width), BF16),
            pltpu.VMEM((2, rows.shape[0] // 128, 2 * units, 128), F32),
            pltpu.VMEM((count, rows.shape[0], units), BF16),
            pltpu.SemaphoreType.DMA((len(pieces),)),
        ],
        compiler_params=pltpu.CompilerParams(vmem_limit_bytes=52 << 20),
        cost_estimate=pl.CostEstimate(
            flops=6 * rows.shape[0] * width * units * count,
            bytes_accessed=6 * width * units * count,
            transcendentals=rows.shape[0] * units * count,
        ),
        name="experts",
    )(rows, *pieces)


def shards(
    tokens,
    norm_gain,
    w_qkv,
    w_out,
    moe_gain,
    w_router,
    gate_up,
    w_down,
    lengths,
    blocks_seen,
    expert_ids,
    old_place,
    new_place,
):
    block_rows = tokens.shape[0]
    model_width = tokens.shape[1]
    exp_count = lax.axis_size(EXP)
    block_index = lax.axis_index(SEQ)
    slot_index = lax.axis_index(EXP)
    heads_here = w_qkv.shape[2] // HEAD_DIM
    slice_width = gate_up.shape[3]
    shard_rows = block_rows // exp_count
    n_zh, n_x, n_c = lax.axis_size("zh"), lax.axis_size("x"), lax.axis_size("c")
    my_zh, my_x, my_c = lax.axis_index("zh"), lax.axis_index("x"), lax.axis_index("c")
    expert_count = w_router.shape[1]
    expert_range = jnp.arange(expert_count, dtype=I32)

    where = jnp.stack([my_zh, my_x, my_c]).astype(I32)

    by_unit = jnp.transpose(gate_up[0], (2, 0, 1))
    down = w_down[0]
    half = (slice_width + slice_width // 2) // 2
    first_rows = by_unit[:half]
    second_rows = second_half(by_unit, down, half)
    first_left, first_right = shift(first_rows, "x", 1), shift(first_rows, "x", -1)

    slot_old = owner_table(old_place)
    source_slot = jnp.sum(
        jnp.where(new_place[:, None] == expert_range[None, :], slot_old[None, :], 0),
        axis=1,
        dtype=I32,
    )

    def pad_pieces(array, piece):
        spare = exp_count * piece - array.shape[0]
        padded = jnp.pad(array, ((0, spare),) + ((0, 0),) * (array.ndim - 1))
        return padded.reshape((exp_count, piece) + array.shape[1:])

    def spread_pieces(array, piece):
        return lax.all_to_all(pad_pieces(array, piece), EXP, 0, 0, tiled=True)

    down_spread = spread_pieces(down, -(-slice_width // (8 * exp_count)) * 8)

    row_ids = block_index * block_rows + jnp.arange(block_rows, dtype=I32)[:, None]
    docs = jnp.arange(lengths.shape[0], dtype=I32)
    ending = jnp.sum(jnp.where(docs[None, :] <= docs[:, None], lengths[None, :], 0), axis=1)
    starts = jnp.max(jnp.where(row_ids >= ending[None, :], ending[None, :], 0), axis=1)[:, None]
    lanes = jnp.arange(128, dtype=I32)[None, :]
    spacing = (lanes % (HEAD_DIM // 2)).astype(F32) / (HEAD_DIM // 2)
    angles = (row_ids - starts).astype(F32) * jnp.exp(-jnp.log(10000.0) * spacing)
    cosine = jnp.cos(angles)
    sine = jnp.where(lanes % HEAD_DIM < HEAD_DIM // 2, -1.0, 1.0) * jnp.sin(angles)
    unseen = jnp.where(blocks_seen > 0, 0.0, masked_score)
    unseen = jnp.broadcast_to(unseen, (block_rows, unseen.shape[1]))
    ids_lanes = jnp.pad(
        expert_ids.astype(F32),
        ((0, block_rows - shard_rows), (0, HEAD_DIM - unseen.shape[1] - 2)),
    )
    extra = jnp.concatenate([jnp.zeros((block_rows, HEAD_DIM), F32), unseen, ids_lanes], axis=1)
    packed = project(
        where,
        tokens,
        norm_gain,
        jnp.transpose(w_qkv, (1, 0, 2)),
        cosine,
        sine,
        extra,
    )

    packets = [packed[0]] + [shift(packed[step], "zh", step) for step in range(1, n_zh)]
    pairs, queries, ids_rows = join_packets(packets, shard_rows)
    gate_piece = -(-slice_width // exp_count)
    pairs, first_left, first_right, gate_pieces, down_spread = tie(
        pairs, first_left, first_right, pad_pieces(by_unit, gate_piece), down_spread
    )
    gate_spread = lax.all_to_all(gate_pieces, EXP, 0, 0, tiled=True)
    near = jnp.concatenate(gather_near(pairs, "x"), axis=0)
    near, second_rows = tie(near, second_rows)
    second_left, second_right = shift(second_rows, "x", 1), shift(second_rows, "x", -1)
    other = shift(near, "c", 1)
    attended = attend(where, lengths, queries, near, other, n_zh, n_x, n_c)
    attended, gate_spread = tie(attended, gate_spread)
    returned = [attended[0]] + [shift(attended[step], "zh", -step) for step in range(1, n_zh)]
    partial = output_projection(where, w_out, returned)
    partial = partial.reshape(exp_count, shard_rows, model_width)
    partial, first_left, second_left, second_right = tie(
        partial, first_left, second_left, second_right
    )
    first_far, second_far = shift(first_left, "x", 1), shift(second_right, "x", -1)

    partial = lax.all_to_all(partial, EXP, 0, 0, tiled=True)
    first_other, second_other = shift(first_rows, "c", 1), shift(second_rows, "c", 1)
    partial, first_other, second_other = tie(partial, first_other, second_other)
    head_total = jnp.sum(partial.astype(F32), axis=0)
    residual = lax.dynamic_slice_in_dim(tokens, slot_index * shard_rows, shard_rows, 0)
    hidden = (residual.astype(F32) + head_total).astype(BF16)
    moe_in = rms_scale(hidden, moe_gain).astype(BF16)

    rows_near = jnp.concatenate(gather_near(moe_in, "zh"), axis=0)
    ids_near = ids_rows[:, 96:98].astype(F32).astype(I32)
    capacity = min(shard_rows, 4 * shard_rows // exp_count)
    near_rows = n_zh * shard_rows
    pair_ids = ids_near.reshape(n_zh, 2 * shard_rows)
    pair_marks = (pair_ids[:, :, None] == expert_range[None, None, :]).astype(I32)
    earlier = jnp.cumsum(pair_marks, axis=1, dtype=I32) - pair_marks
    rank_in = jnp.sum(earlier * pair_marks, axis=2, dtype=I32)
    owner_of = jnp.sum(pair_marks * slot_old[None, None, :], axis=2, dtype=I32)
    target = (owner_of * n_zh + jnp.arange(n_zh, dtype=I32)[:, None]) * capacity + rank_in
    target = target.reshape(near_rows, 2)
    slot_range = jnp.arange(exp_count * n_zh * capacity, dtype=I32)
    marks = target[:, :, None] == slot_range[None, None, :]
    selector = jnp.any(marks, axis=1).astype(BF16)
    outgoing = lax.dot_general(
        selector, rows_near, (((0,), (0,)), ((), ())), preferred_element_type=F32
    ).astype(BF16)
    ordered = reorder(source_slot, gate_spread, down_spread)
    outgoing, ordered, first_far, second_far = tie(outgoing, ordered, first_far, second_far)
    sets = [
        (first_rows, second_rows),
        (first_left, second_left),
        (first_right, second_right),
        (first_far, second_far),
    ]
    sets_other = [(first_other, second_other)]
    sets_other += [tuple(shift(piece, "c", 1) for piece in pieces) for pieces in sets[1:]]
    arrived = lax.all_to_all(
        outgoing.reshape(exp_count, n_zh * capacity, model_width), EXP, 0, 0, tiled=True
    ).reshape(-1, model_width)

    logits = jnp.dot(rows_near, w_router, preferred_element_type=F32)
    chosen = jnp.sum(
        jnp.where(ids_near[:, :, None] == expert_range[None, None, :], logits[:, None, :], 0.0),
        axis=2,
    )
    gate_first = 1.0 / (1.0 + jnp.exp(chosen[:, 1] - chosen[:, 0]))
    gate_second = 1.0 / (1.0 + jnp.exp(chosen[:, 0] - chosen[:, 1]))
    gating = jnp.stack([gate_first, gate_second], axis=1)
    spread = jnp.sum(jnp.where(marks, gating[:, :, None], 0.0), axis=1)

    arrived, ordered = tie(arrived, ordered)
    moved = lax.all_to_all(ordered, EXP, 0, 0, tiled=True)
    parts = run_experts(arrived, sets + sets_other, slice_width)
    parts, moved = tie(parts, moved)
    back = lax.all_to_all(
        parts.reshape(exp_count, n_zh * capacity, model_width), EXP, 0, 0, tiled=True
    ).reshape(-1, model_width)
    combined = jnp.dot(spread, back.astype(F32), precision=lax.Precision.HIGHEST)
    combined = combined.astype(BF16)
    combined = combined.reshape(n_zh, shard_rows, model_width)
    moe_sum = combined[0].astype(F32)
    for step in range(1, n_zh):
        moe_sum = moe_sum + shift(combined[step], "zh", -step).astype(F32)
    layer_out = (hidden.astype(F32) + moe_sum).astype(BF16)

    new_gate = moved[:, :gate_piece].reshape(-1, 2, model_width)[:slice_width]
    new_down = moved[:, gate_piece:].reshape(-1, model_width)[:slice_width]
    new_gate_up, new_down = jnp.transpose(new_gate, (1, 2, 0))[None], new_down[None]
    return (layer_out, new_gate_up, new_down)


def solution(mesh):
    fine = Mesh(mesh.devices.reshape(4, 4, 2, 2, 4), SEQ + EXP)
    in_specs = (
        P(SEQ, None),
        P(),
        P(None, None, EXP),
        P(EXP, None),
        P(),
        P(),
        P(EXP, None, None, SEQ),
        P(EXP, SEQ, None),
        P(),
        P(SEQ, None),
        P(SEQ + EXP, None),
        P(),
        P(),
    )
    out_specs = (P(SEQ + EXP, None), P(EXP, None, None, SEQ), P(EXP, SEQ, None))
    return jax.shard_map(shards, mesh=fine, in_specs=in_specs, out_specs=out_specs, check_vma=False)
```
